32 devices in a mesh: dp: 4 (over z), ctx: 2 (over x), tp: 4 (over y, core).
Axes of the slice: x: 2, y: 2, z: 4, core: 2. Of those that a mesh axis runs over, the one named last changes fastest.
Arguments:
- tokens: bfloat16 [512, 2048], P(('dp', 'ctx', 'tp')), may hold values from -6 to 6
- grad_out: bfloat16 [512, 2048], P(('dp', 'ctx', 'tp')), may hold values from -6 to 6
- expert_ids: int32 [512, 8], P(('dp', 'ctx')), may hold values from 0 to 63, all different within a row; in each aligned block of 64 rows (0 to 63, 64 to 127, ...) at most 16 rows name the same one
- router_weights: bfloat16 [512, 8], P(('dp', 'ctx')), may hold values from 0.029907227 to 0.3984375
- w_gate: bfloat16 [64, 2048, 1536], P(('dp', 'ctx'), None, 'tp'), may hold values from -0.125 to 0.125
- w_up: bfloat16 [64, 2048, 1536], P(('dp', 'ctx'), None, 'tp'), may hold values from -0.125 to 0.125
- w_down: bfloat16 [64, 1536, 2048], P(('dp', 'ctx'), 'tp'), may hold values from -0.15625 to 0.15625
Outputs:
- layer_out: bfloat16 [512, 2048], P(('dp', 'ctx', 'tp'))
- grad_tokens: bfloat16 [512, 2048], P(('dp', 'ctx', 'tp'))
- grad_w_gate: bfloat16 [64, 2048, 1536], P(('dp', 'ctx'), None, 'tp')
- grad_w_up: bfloat16 [64, 2048, 1536], P(('dp', 'ctx'), None, 'tp')
- grad_w_down: bfloat16 [64, 1536, 2048], P(('dp', 'ctx'), 'tp')
The draws below stay inside these ranges and needn't reach their ends.
Inputs may be any that keep to these rules, and one draw needn't show every extreme that they name: `expert_ids`: each row names 8 different experts. Among the tokens of one index of dp and ctx no expert is named by more than 16 of them, and in every draw some expert is named by exactly 16 of them.
All inputs are finite; a program needn't handle non-finite values.
Results may differ from the reference program's by a relative error of at most 0.012.
Values may be sent and summed in bfloat16 or wider, within the bound.
A program may use at most 384 MiB of HBM per device.

```python
import math
import jax
import jax.numpy as jnp
import numpy as np
from jax import lax

D = 2048
FF = 1536
EXPERTS = 64
TOPK = 8
TOK_DEV = 16
MOST = 16
TOKENS = 512
N_DP = 4
N_CTX = 2
N_TP = 4


def level_of(stream_key, shape, split, smallest, largest):
    factor_of, own = 1.0, jax.random.fold_in(stream_key, 6)
    for dim, blocks in split:
        heights = jnp.exp(jax.random.uniform(jax.random.fold_in(own, dim), (blocks,), jnp.float32, smallest / len(split), largest / len(split)))
        factor_of = factor_of * jnp.repeat(heights, shape[dim] // blocks).reshape([-1 if axis == dim else 1 for axis in range(len(shape))])
    return factor_of


def assign_block(own_key, own, number, rows, count, top, bound, slope):
    sequence = jax.random.permutation(own_key, count)
    packed, usual = load_shares(count, rows * top, bound, slope, True), load_shares(count, rows * top, bound, slope, False)
    places = jnp.arange(count)

    def named(sizes, offset_by):
        used = int((sizes > 0).sum())
        fixed = max(1, used // 4)
        moved = fixed + (places - fixed + offset_by * (used - fixed)) % max(1, count - fixed)
        return jnp.zeros((count,), jnp.int32).at[sequence[jnp.where(places < fixed, places, moved)]].set(jnp.asarray(sizes, jnp.int32))

    sizes = jnp.where(number % 4 == 0, named(packed, number // 4), named(usual, number - number // 4 - 1))
    mixed = jax.random.permutation(jax.random.fold_in(own, 3), count)
    donor, taker = mixed[0:count // 2 * 2:2], mixed[1:count // 2 * 2:2]
    slack = jnp.minimum(sizes[donor] - 1, bound - sizes[taker]) // 2
    slack = jnp.where((donor == sequence[0]) | (taker == sequence[0]) | (sizes[taker] == 0), 0, jnp.maximum(slack, 0))
    moved = jax.random.randint(jax.random.fold_in(own, 4), (count // 2,), 0, 1 << 20) % (slack + 1)
    sizes = sizes.at[donor].add(-moved).at[taker].add(moved)
    members = jnp.searchsorted(jnp.cumsum(sizes), jnp.arange(rows * top), side="right").astype(jnp.int32)
    table = members.reshape(top, rows).T
    table = table[jax.random.permutation(jax.random.fold_in(own, 1), rows)]
    offset_by = jax.random.randint(jax.random.fold_in(own, 2), (rows, 1), 0, top)
    return jnp.take_along_axis(table, (jnp.arange(top)[None, :] + offset_by) % top, axis=1)


def load_shares(count, total, most, slope, full):
    weights = [(1 << 20) // math.isqrt(rank ** slope) + 1 for rank in range(1, count + 1)]
    largest = most if full else min(most, max(-(-total // count), total * weights[0] // sum(weights)))
    least = 1 if total - largest >= count - 1 else 0
    counts, rest = [largest] + [least] * (count - 1), total - largest - least * (count - 1)
    while rest > 0:
        candidates = [i for i in range(1, count) if counts[i] < largest] or [i for i in range(1, count) if counts[i] < most]
        pool, remaining = sum([weights[i] for i in candidates]), rest
        for i in candidates:
            addition = min(most - counts[i], max(1, remaining * weights[i] // pool), rest)
            counts[i] = counts[i] + addition
            rest = rest - addition
    return np.array(counts)


def normal_values(key, dims, width, reach, shards=(), kind=jnp.bfloat16):
    values = width * jax.random.normal(key, dims, jnp.float32)
    if shards:
        values = values * level_of(key, dims, shards, -0.22, 0.18)
    return jnp.clip(values, -reach, reach).astype(kind)


def setup_inputs(seed: int = 0) -> dict:
    key_of = jax.random.split(jax.random.key(seed), 8)
    tokens = normal_values(key_of[0], (TOKENS, D), 1.0, 6.0, ((0, 32),))
    grad_out = normal_values(key_of[1], (TOKENS, D), 1.0, 6.0, ((0, 32),))
    expert_ids_keys = jax.random.split(jax.random.fold_in(key_of[2], 1), TOKENS // (TOK_DEV * N_TP))
    expert_ids_turns = jax.random.permutation(jax.random.fold_in(key_of[2], 3), TOKENS // (TOK_DEV * N_TP))
    expert_ids = jax.vmap(lambda own, number: assign_block(jax.random.fold_in(key_of[2], 2), own, number, TOK_DEV * N_TP, EXPERTS, TOPK, MOST, 2))(expert_ids_keys, expert_ids_turns).reshape((TOKENS, TOPK))
    router_weights = jnp.clip(jnp.exp(math.log(0.3984375) - 2.5894505 * jax.random.uniform(key_of[3], (TOKENS, TOPK), jnp.float32) ** level_of(key_of[3], (TOKENS, TOPK), ((0, 8),), -0.2, 0.2)), 0.029907227, 0.3984375).astype(jnp.bfloat16)
    w_gate = normal_values(key_of[4], (EXPERTS, D, FF), D ** -0.5, 0.125, ((0, 8), (2, 4)))
    w_up = normal_values(key_of[5], (EXPERTS, D, FF), D ** -0.5, 0.125, ((0, 8), (2, 4)))
    w_down = normal_values(key_of[6], (EXPERTS, FF, D), FF ** -0.5, 0.15625, ((0, 8), (1, 4)))
    return dict(tokens=tokens, grad_out=grad_out, expert_ids=expert_ids, router_weights=router_weights, w_gate=w_gate, w_up=w_up, w_down=w_down)


def slot_ranks(group_ids):
    onehot = (group_ids[:, None] == jnp.arange(EXPERTS, dtype=jnp.int32)[None, :]).astype(jnp.int32)
    earlier = jnp.cumsum(onehot, axis=0) - onehot
    return jnp.sum(earlier * onehot, axis=1).astype(jnp.int32)


def round_trip(values):
    return lax.optimization_barrier(values.astype(jnp.bfloat16)).astype(jnp.float32)


def expert_pass(operands):
    inputs, cotangent, weights, gate_w, up_w, down_w = operands
    hidden_share = FF // N_TP
    gate = jnp.dot(inputs, gate_w, preferred_element_type=jnp.float32)
    upward = jnp.dot(inputs, up_w, preferred_element_type=jnp.float32)
    sigmoid_gate = jax.nn.sigmoid(gate)
    row_scale = weights.astype(jnp.float32)[:, None]
    activation = (row_scale * gate * sigmoid_gate * upward).astype(jnp.bfloat16)
    parts = jnp.einsum("rjf,jfd->rjd", activation.reshape(-1, N_TP, hidden_share).astype(jnp.float32),
                       down_w.reshape(N_TP, hidden_share, D).astype(jnp.float32))
    output_rows = jnp.sum(round_trip(parts), axis=1)
    backward = lax.dot_general(cotangent, down_w, (((1,), (1,)), ((), ())), preferred_element_type=jnp.float32)
    grad_gate_pre = (backward * row_scale * upward * sigmoid_gate * (1.0 + gate * (1.0 - sigmoid_gate))).astype(jnp.bfloat16)
    grad_up_pre = (backward * row_scale * gate * sigmoid_gate).astype(jnp.bfloat16)
    grad_down = lax.dot_general(activation, cotangent, (((0,), (0,)), ((), ())), preferred_element_type=jnp.float32).astype(jnp.bfloat16)
    grad_gate = lax.dot_general(inputs, grad_gate_pre, (((0,), (0,)), ((), ())), preferred_element_type=jnp.float32).astype(jnp.bfloat16)
    grad_up = lax.dot_general(inputs, grad_up_pre, (((0,), (0,)), ((), ())), preferred_element_type=jnp.float32).astype(jnp.bfloat16)
    input_parts = jnp.einsum("rjf,djf->rjd", grad_gate_pre.reshape(-1, N_TP, hidden_share).astype(jnp.float32),
                             gate_w.reshape(D, N_TP, hidden_share).astype(jnp.float32))
    input_parts = input_parts + jnp.einsum("rjf,djf->rjd", grad_up_pre.reshape(-1, N_TP, hidden_share).astype(jnp.float32),
                                           up_w.reshape(D, N_TP, hidden_share).astype(jnp.float32))
    input_rows = jnp.sum(round_trip(input_parts), axis=1)
    return output_rows, input_rows, grad_gate, grad_up, grad_down


def reference(tokens, grad_out, expert_ids, router_weights, w_gate, w_up, w_down):
    group_rows = TOK_DEV * N_TP
    group_count = N_DP * N_CTX
    expert_rows = group_count * MOST
    grouped = expert_ids.reshape(group_count, group_rows * TOPK)
    ranks = lax.map(slot_ranks, grouped)
    group_index = jnp.arange(group_count, dtype=jnp.int32)[:, None]
    slots = (grouped * expert_rows + group_index * MOST + ranks).astype(jnp.int32).reshape(TOKENS, TOPK)
    assignments = TOKENS * TOPK
    source = jnp.full((EXPERTS * expert_rows,), assignments, jnp.int32).at[slots.reshape(-1)].set(
        jnp.arange(assignments, dtype=jnp.int32))
    token_of = source // TOPK
    padded_tokens = jnp.concatenate([tokens, jnp.zeros((1, D), jnp.bfloat16)], axis=0)
    padded_grads = jnp.concatenate([grad_out, jnp.zeros((1, D), jnp.bfloat16)], axis=0)
    padded_weights = jnp.concatenate([router_weights.reshape(-1), jnp.zeros((1,), jnp.bfloat16)], axis=0)
    inputs = padded_tokens[token_of].reshape(EXPERTS, expert_rows, D)
    cotangents = padded_grads[token_of].reshape(EXPERTS, expert_rows, D)
    scales = padded_weights[source].reshape(EXPERTS, expert_rows)
    results = lax.map(expert_pass, (inputs, cotangents, scales, w_gate, w_up, w_down))
    output_table = results[0].reshape(EXPERTS * expert_rows, D)
    input_table = results[1].reshape(EXPERTS * expert_rows, D)

    def combine(table):
        def add_pick(running, column):
            return running + table[column], None
        summed, unused = lax.scan(add_pick, jnp.zeros((TOKENS, D), jnp.float32), slots.T)
        return summed.astype(jnp.bfloat16)

    return combine(output_table), combine(input_table), results[2], results[3], results[4]
```

```python
import jax
import jax.numpy as jnp
from jax import lax
from jax.experimental import pallas as pl
from jax.experimental.pallas import tpu as pltpu
from jax.sharding import PartitionSpec as P

contract_last = (((1,), (1,)), ((), ()))
contract_first = (((0,), (0,)), ((), ()))


def swiglu_rows(inputs, cotangent, row_weights, gate_w, up_w, down_w):
    gate = jnp.dot(inputs, gate_w, preferred_element_type=jnp.float32)
    upward = jnp.dot(inputs, up_w, preferred_element_type=jnp.float32)
    sigmoid_gate = jax.nn.sigmoid(gate)
    row_scale = row_weights.astype(jnp.float32)[:, None]
    activation = (row_scale * gate * sigmoid_gate * upward).astype(jnp.bfloat16)
    output_rows = jnp.dot(activation, down_w, preferred_element_type=jnp.float32).astype(
        jnp.bfloat16
    )
    backward = lax.dot_general(cotangent, down_w, contract_last, preferred_element_type=jnp.float32)
    grad_gate_pre = (
        backward * row_scale * upward * sigmoid_gate * (1.0 + gate * (1.0 - sigmoid_gate))
    ).astype(jnp.bfloat16)
    grad_up_pre = (backward * row_scale * gate * sigmoid_gate).astype(jnp.bfloat16)
    input_rows = (
        lax.dot_general(grad_gate_pre, gate_w, contract_last, preferred_element_type=jnp.float32)
        + lax.dot_general(grad_up_pre, up_w, contract_last, preferred_element_type=jnp.float32)
    ).astype(jnp.bfloat16)
    grad_down = lax.dot_general(
        activation, cotangent, contract_first, preferred_element_type=jnp.float32
    )
    grad_gate = lax.dot_general(
        inputs, grad_gate_pre, contract_first, preferred_element_type=jnp.float32
    )
    grad_up = lax.dot_general(
        inputs, grad_up_pre, contract_first, preferred_element_type=jnp.float32
    )
    return (output_rows, input_rows, grad_gate, grad_up, grad_down)


def shards(tokens, grad_out, expert_ids, router_weights, w_gate, w_up, w_down):
    expert_devices = lax.axis_size(("dp", "ctx"))
    group_rows, top_count = expert_ids.shape
    local_experts = w_gate.shape[0]
    expert_total = expert_devices * local_experts
    slot_most = 2 * group_rows * top_count // expert_total
    model_width = tokens.shape[1]
    group_tokens, group_grads = (
        lax.all_to_all(tokens, "tp", split_axis=1, concat_axis=0, tiled=True),
        lax.all_to_all(grad_out, "tp", split_axis=1, concat_axis=0, tiled=True),
    )
    carried = group_tokens.shape[1]
    flat_ids = expert_ids.reshape(-1)
    onehot = (flat_ids[:, None] == jnp.arange(expert_total, dtype=jnp.int32)[None, :]).astype(
        jnp.int32
    )
    place = jnp.arange(flat_ids.shape[0], dtype=jnp.int32)
    before = (place[:, None] > place[None, :]).astype(jnp.bfloat16)
    earlier = jnp.dot(
        before, onehot.astype(jnp.bfloat16), preferred_element_type=jnp.float32
    ).astype(jnp.int32)
    ranks = jnp.sum(earlier * onehot, axis=1)
    slots = flat_ids * slot_most + ranks
    assignments = group_rows * top_count
    source = (
        jnp.full((expert_total * slot_most,), assignments, jnp.int32)
        .at[slots]
        .set(jnp.arange(assignments, dtype=jnp.int32))
    )
    token_of = source // top_count
    zero_row = jnp.zeros((1, carried), jnp.bfloat16)
    send_tokens = jnp.concatenate([group_tokens, zero_row], axis=0)[token_of].reshape(
        expert_devices, local_experts * slot_most, carried
    )
    send_grads = jnp.concatenate([group_grads, zero_row], axis=0)[token_of].reshape(
        expert_devices, local_experts * slot_most, carried
    )
    send_weights = jnp.concatenate(
        [router_weights.reshape(-1), jnp.zeros((1,), jnp.bfloat16)], axis=0
    )[source].reshape(expert_devices, local_experts * slot_most)
    recv_tokens, recv_grads, recv_weights = (
        lax.all_to_all(send_tokens, ("dp", "ctx"), split_axis=0, concat_axis=0, tiled=True),
        lax.all_to_all(send_grads, ("dp", "ctx"), split_axis=0, concat_axis=0, tiled=True),
        lax.all_to_all(send_weights, ("dp", "ctx"), split_axis=0, concat_axis=0, tiled=True),
    )
    recv_tokens, recv_grads = (
        lax.all_gather(recv_tokens, "tp", axis=2, tiled=True),
        lax.all_gather(recv_grads, "tp", axis=2, tiled=True),
    )
    token_grid = recv_tokens.reshape(expert_devices, local_experts, slot_most, model_width)
    grad_grid = recv_grads.reshape(expert_devices, local_experts, slot_most, model_width)
    weight_grid = recv_weights.reshape(expert_devices, local_experts, slot_most)
    outputs = []
    for expert_index in range(local_experts):
        outputs.append(
            swiglu_rows(
                token_grid[:, expert_index].reshape(-1, model_width),
                grad_grid[:, expert_index].reshape(-1, model_width),
                weight_grid[:, expert_index].reshape(-1),
                w_gate[expert_index],
                w_up[expert_index],
                w_down[expert_index],
            )
        )
    out_rows = jnp.stack(
        [entry[0].reshape(expert_devices, slot_most, model_width) for entry in outputs], axis=1
    ).reshape(expert_devices, local_experts * slot_most, model_width)
    in_rows = jnp.stack(
        [entry[1].reshape(expert_devices, slot_most, model_width) for entry in outputs], axis=1
    ).reshape(expert_devices, local_experts * slot_most, model_width)
    grad_gate = jnp.stack([entry[2] for entry in outputs], axis=0).astype(jnp.bfloat16)
    grad_up = jnp.stack([entry[3] for entry in outputs], axis=0).astype(jnp.bfloat16)
    grad_down = jnp.stack([entry[4] for entry in outputs], axis=0).astype(jnp.bfloat16)
    slot_grid = slots.reshape(group_rows, top_count)

    def combine(table):
        picked = table.reshape(expert_total * slot_most, -1)[slot_grid]
        return jnp.sum(picked, axis=1)

    column_out, column_in = (
        lax.psum_scatter(
            out_rows.astype(jnp.float32).astype(jnp.bfloat16), "tp", scatter_dimension=2, tiled=True
        ).astype(jnp.float32),
        lax.psum_scatter(
            in_rows.astype(jnp.float32).astype(jnp.bfloat16), "tp", scatter_dimension=2, tiled=True
        ).astype(jnp.float32),
    )
    back_out, back_in = (
        lax.all_to_all(
            column_out.astype(jnp.bfloat16), ("dp", "ctx"), split_axis=0, concat_axis=0, tiled=True
        ).astype(column_out.dtype),
        lax.all_to_all(
            column_in.astype(jnp.bfloat16), ("dp", "ctx"), split_axis=0, concat_axis=0, tiled=True
        ).astype(column_in.dtype),
    )
    layer_out, grad_tokens = (
        lax.all_to_all(
            combine(back_out).astype(jnp.bfloat16), "tp", split_axis=0, concat_axis=1, tiled=True
        ).astype(jnp.float32),
        lax.all_to_all(
            combine(back_in).astype(jnp.bfloat16), "tp", split_axis=0, concat_axis=1, tiled=True
        ).astype(jnp.float32),
    )
    return (
        layer_out.astype(jnp.bfloat16),
        grad_tokens.astype(jnp.bfloat16),
        grad_gate,
        grad_up,
        grad_down,
    )


def split_at(total, most):
    size = most
    while total % size:
        size //= 2
    return size


class Place:
    def __init__(self):
        self.ring = lax.axis_size("dp")
        self.z, self.x = lax.axis_index("dp"), lax.axis_index("ctx")
        tp = lax.axis_index("tp")
        self.y, self.c = tp // 2, tp % 2

    def device(self, z=None, x=None, y=None, c=None):
        pick = lambda value, own: own if value is None else value
        tp = pick(y, self.y) * 2 + pick(c, self.c)
        return (pick(z, self.z), pick(x, self.x), tp)

    def ahead(self, k):
        return self.device(z=lax.rem(self.z + k, self.ring))

    def core_peer(self):
        return self.device(c=1 - self.c)

    def x_peer(self):
        return self.device(x=1 - self.x)

    def y_peer(self):
        return self.device(y=1 - self.y)

    def greet(self):
        barrier = pltpu.get_barrier_semaphore()
        others = [self.core_peer(), self.x_peer(), self.y_peer()]
        others += [self.ahead(k) for k in range(1, self.ring)]
        for other in others:
            pl.semaphore_signal(
                barrier, inc=1, device_id=other, device_id_type=pl.DeviceIdType.MESH
            )
        return lambda: pl.semaphore_wait(barrier, len(others))


def layer_kernel(
    tok, grd, ids, weights, gate_w, up_w, down_w,
    inputs_out, cotangent_out, act_out, pre_out, layer_out, grad_out,
    tab, routes, wide, down, rows, wide_acc, back_acc, act, pre, pick, place, scale,
    got1, got2, got3, got4,
    own_sem, weight_sem, row_sem, hidden_sem,
    route_send, route_recv, along_send, along_recv, own_send, own_recv, part_send, part_recv,
    red_send, red_recv,
):
    f32, bf16, i32 = jnp.float32, jnp.bfloat16, jnp.int32
    at = Place()
    x, y, c, ring = at.x, at.y, at.c, at.ring
    chunks, step = tab.shape[0], tab.shape[-1]
    own_count = tab.shape[-2]
    experts, hidden, width = down.shape
    half_rows = rows.shape[3] // 2
    token_half = pick.shape[2]
    half_ring = ring // 2
    all_rows = experts * half_rows
    group_rows = ids.shape[0]
    cols = lambda n, size: pl.ds(n * size, size)

    def send(source, target, send_sem, recv_sem, device):
        copy = pltpu.make_async_remote_copy(
            src_ref=source, dst_ref=target, send_sem=send_sem, recv_sem=recv_sem,
            device_id=device, device_id_type=pl.DeviceIdType.MESH,
        )
        copy.start()
        return copy

    def local(source, target, sem):
        copy = pltpu.make_async_copy(source, target, sem)
        copy.start()
        return copy

    sent = []
    met = at.greet()
    own_loads = [
        local(table.at[:, cols(n, step)], tab.at[n, h, 0, x, y, c], own_sem.at[n, h])
        for n in range(chunks)
        for h, table in enumerate((tok, grd))
    ]
    weight_loads = [
        (
            local(gate_w.at[:, cols(n, step)], wide.at[:, cols(n, step), pl.ds(0, hidden)],
                  weight_sem.at[n, 0]),
            local(up_w.at[:, cols(n, step)], wide.at[:, cols(n, step), pl.ds(hidden, hidden)],
                  weight_sem.at[n, 1]),
            local(down_w.at[:, :, cols(n, step)], down.at[:, :, cols(n, step)],
                  weight_sem.at[n, 2]),
        )
        for n in range(chunks)
    ]
    top = ids.shape[1]
    routes[0, x] = jnp.zeros(routes.shape[2:], bf16)
    routes[0, x, :, 0:top] = ids[...].astype(f32).astype(bf16)
    routes[0, x, :, top : 2 * top] = weights[...]
    for copy in own_loads:
        copy.wait()
    met()

    route_along = [
        send(routes.at[0, x], routes.at[ring - k, x], route_send.at[k], route_recv.at[k],
             at.ahead(k))
        for k in range(1, ring)
    ]
    peers = ((at.x_peer(), at.y_peer()), (at.y_peer(), at.x_peer()))

    def stage_ref(lead, h, stage):
        if stage == 0:
            return tab.at[(*lead, x, y, c)]
        if stage == 1:
            return tab.at[(*lead, slice(None), y, c)] if h == 0 else tab.at[(*lead, x, slice(None), c)]
        return tab.at[(*lead, slice(None), slice(None), c)]

    def own_stage(h, stage):
        ref = stage_ref((slice(None), h, 0), h, stage)
        peer = at.core_peer() if stage == 2 else peers[h][stage]
        return send(ref, ref, own_send.at[h, stage], own_recv.at[h, stage], peer)

    def part_stage(n, h, stage):
        ref = stage_ref((n, h, pl.ds(1, ring - 1)), h, stage)
        peer = at.core_peer() if stage == 2 else peers[h][stage]
        return send(ref, ref, part_send.at[n, h, stage], part_recv.at[n, h, stage], peer)

    owns = [[own_stage(h, 0)] for h in range(2)]
    along = [
        [
            send(tab.at[n, h, 0, x, y, c], tab.at[n, h, ring - k, x, y, c],
                 along_send.at[n, h, k], along_recv.at[n, h, k], at.ahead(k))
            for k in range(1, ring)
            for h in range(2)
        ]
        for n in range(chunks)
    ]
    for copy in route_along:
        copy.wait_recv()
    route_across = send(routes.at[:, x], routes.at[:, x], route_send.at[0], route_recv.at[0],
                        at.x_peer())
    for stage in (1, 2):
        for h in range(2):
            owns[h][-1].wait_recv()
            owns[h].append(own_stage(h, stage))
    parts = {}

    def enter(n):
        for copy in along[n]:
            copy.wait_recv()
        for h in range(2):
            parts[n, h, 0] = part_stage(n, h, 0)

    def advance(n, stage):
        for h in range(2):
            parts[n, h, stage - 1].wait_recv()
            parts[n, h, stage] = part_stage(n, h, stage)

    enter(0)
    route_across.wait_recv()
    first = lax.axis_index(("dp", "ctx")) * experts
    table = routes[...].reshape(ring * 2 * group_rows, routes.shape[-1]).astype(f32)
    flipped = table.T
    total = flipped.shape[1]
    named_ids = flipped[0:top]
    named_weights = flipped[top : 2 * top]
    hits, scales = [], []
    for e in range(experts):
        named = named_ids == (first + e).astype(f32)
        hits.append(jnp.max(jnp.where(named, 1.0, 0.0), axis=0, keepdims=True))
        scales.append(jnp.sum(jnp.where(named, named_weights, 0.0), axis=0, keepdims=True))
    before = (
        lax.broadcasted_iota(i32, (token_half, token_half), 0)
        < lax.broadcasted_iota(i32, (token_half, token_half), 1)
    )
    before = jnp.where(before, 1.0, 0.0).astype(bf16)
    hit_all = jnp.concatenate(hits, axis=0)
    spots = lax.broadcasted_iota(i32, (half_rows, token_half), 0).astype(f32)
    for half in range(2):
        here = slice(half * token_half, (half + 1) * token_half)
        hit = hit_all[:, here]
        rank = jnp.dot(hit.astype(bf16), before, preferred_element_type=f32)
        order = jnp.where(hit > 0.5, rank, -1.0)
        for e in range(experts):
            chosen = spots == order[e : e + 1]
            pick[half, e * half_rows : (e + 1) * half_rows] = jnp.where(chosen, 1.0, 0.0).astype(bf16)
            scale[e, half * half_rows : (half + 1) * half_rows] = jnp.broadcast_to(
                jnp.sum(jnp.where(chosen, scales[e][:, here], 0.0), axis=1, keepdims=True),
                (half_rows, scale.shape[2]),
            )
        place[half] = pick[half].astype(f32).T.astype(bf16)
    advance(0, 1)
    if chunks > 1:
        enter(1)

    row_saves = []
    for n in range(chunks):
        if n + 1 < chunks:
            advance(n + 1, 1)
        if n + 2 < chunks:
            enter(n + 2)
        advance(n, 2)
        if n == 0:
            for h in range(2):
                owns[h][-1].wait_recv()
        for copy in weight_loads[n]:
            copy.wait()
        slot = n % 2
        if n >= 2:
            for copy in row_saves[n - 2]:
                copy.wait()
        for h in range(2):
            parts[n, h, 2].wait_recv()
            for half in range(2):
                block = tab[n, h, half * half_ring : (half + 1) * half_ring].reshape(
                    token_half, step
                )
                picked = jnp.dot(pick[half], block, preferred_element_type=f32).astype(bf16)
                rows[slot, h, :, half * half_rows : (half + 1) * half_rows] = picked.reshape(
                    experts, half_rows, step
                )
        row_saves.append(
            [
                local(rows.at[slot, h], out.at[:, :, cols(n, step)], row_sem.at[slot, h])
                for h, out in enumerate((inputs_out, cotangent_out))
            ]
        )

        @pl.loop(0, experts, unroll=experts)
        def _(e):
            value = jnp.dot(rows[slot, 0, e], wide[e, n * step : (n + 1) * step],
                            preferred_element_type=f32)
            wide_acc[e] = value if n == 0 else wide_acc[e] + value

        @pl.loop(0, experts, unroll=experts)
        def _(e):
            value = lax.dot_general(
                rows[slot, 1, e], down[e, :, n * step : (n + 1) * step], contract_last,
                preferred_element_type=f32,
            )
            back_acc[e] = value if n == 0 else back_acc[e] + value

    @pl.loop(0, experts)
    def _(e):
        gate = wide_acc[e, :, 0:hidden]
        upward = wide_acc[e, :, hidden : 2 * hidden]
        backward = back_acc[e]
        row_scale = scale[e][:, 0:1]
        sigmoid_gate = jax.nn.sigmoid(gate)
        silu = row_scale * gate * sigmoid_gate
        act[e] = (silu * upward).astype(bf16)
        pre[e, :, 0:hidden] = (
            backward * row_scale * upward * sigmoid_gate * (1.0 + gate * (1.0 - sigmoid_gate))
        ).astype(bf16)
        pre[e, :, hidden : 2 * hidden] = (backward * silu).astype(bf16)

    hidden_saves = [local(act, act_out, hidden_sem.at[0]), local(pre, pre_out, hidden_sem.at[1])]
    for copies in row_saves[-2:]:
        for copy in copies:
            copy.wait()
    for copies in (route_along, [route_across], *owns, *along, parts.values()):
        for copy in copies:
            copy.wait_send()

    cuts, cut = got1.shape[0], got1.shape[-1]
    per = step // cut
    red = {}
    back_peers = ((at.y_peer(), at.x_peer()), (at.x_peer(), at.y_peer()))

    def spot(d):
        return d // per, pl.ds((d % per) * cut, cut)

    def reduce_send(d, h, stage, source, target, device):
        red[d, h, stage] = send(
            source, target, red_send.at[d, h, stage], red_recv.at[d, h, stage], device
        )

    def products(d, h):
        n, lanes = spot(d)
        slot = d % 2

        @pl.loop(0, experts, unroll=experts)
        def _(e):
            if h == 0:
                value = jnp.dot(act[e], down[e, :, d * cut : (d + 1) * cut],
                                preferred_element_type=f32)
            else:
                value = lax.dot_general(
                    pre[e], wide[e, d * cut : (d + 1) * cut], contract_last,
                    preferred_element_type=f32,
                )
            rows[slot, h, e, :, 0:cut] = value.astype(bf16)

        for half in range(2):
            block = rows[slot, h, :, half * half_rows : (half + 1) * half_rows, 0:cut].reshape(
                all_rows, cut
            )
            value = jnp.dot(place[half], block, preferred_element_type=f32).astype(bf16)
            tab[n, h, half * half_ring : (half + 1) * half_ring, :, :, :, :, lanes] = value.reshape(
                half_ring, 2, 2, 2, own_count, cut
            )
        reduce_send(d, h, 0, tab.at[n, h, :, :, :, 1 - c, :, lanes], got1.at[d, h], at.core_peer())

    def fold_core(d, h):
        n, lanes = spot(d)
        red[d, h, 0].wait_recv()
        tab[n, h, :, :, :, c, :, lanes] = (
            tab[n, h, :, :, :, c, :, lanes].astype(f32) + got1[d, h].astype(f32)
        ).astype(bf16)
        part = (
            tab.at[n, h, :, :, 1 - y, c, :, lanes] if h == 0 else tab.at[n, h, :, 1 - x, :, c, :, lanes]
        )
        reduce_send(d, h, 1, part, got2.at[d, h], back_peers[h][0])

    def fold_first(d, h):
        n, lanes = spot(d)
        red[d, h, 1].wait_recv()
        mine = (n, h, slice(None), slice(None), y, c) if h == 0 else (n, h, slice(None), x, slice(None), c)
        tab[(*mine, slice(None), lanes)] = (
            tab[(*mine, slice(None), lanes)].astype(f32) + got2[d, h].astype(f32)
        ).astype(bf16)
        part = (
            tab.at[n, h, :, 1 - x, y, c, :, lanes] if h == 0 else tab.at[n, h, :, x, 1 - y, c, :, lanes]
        )
        reduce_send(d, h, 2, part, got3.at[d, h], back_peers[h][1])

    def fold_second(d, h):
        n, lanes = spot(d)
        red[d, h, 2].wait_recv()
        tab[n, h, :, x, y, c, :, lanes] = (
            tab[n, h, :, x, y, c, :, lanes].astype(f32) + got3[d, h].astype(f32)
        ).astype(bf16)
        for k in range(1, ring):
            reduce_send(
                d, h, 2 + k, tab.at[n, h, k, x, y, c, :, lanes], got4.at[d, h, k - 1], at.ahead(k)
            )

    def finish(d, h):
        n, lanes = spot(d)
        total = tab[n, h, 0, x, y, c, :, lanes].astype(f32)
        for k in range(1, ring):
            red[d, h, 2 + k].wait_recv()
            total = total + got4[d, h, k - 1].astype(f32)
        out = layer_out if h == 0 else grad_out
        out[:, d * cut : (d + 1) * cut] = total.astype(bf16)

    for d in range(cuts + 3):
        if d < cuts:
            for h in range(2):
                products(d, h)
        for late, fold in ((3, finish), (2, fold_second), (1, fold_first), (0, fold_core)):
            if 0 <= d - late < cuts:
                for h in range(2):
                    fold(d - late, h)
    for copy in red.values():
        copy.wait_send()
    for copy in hidden_saves:
        copy.wait()


def run_layer(tokens, grad_out, expert_ids, router_weights, w_gate, w_up, w_down, row_count):
    bf16, f32 = jnp.bfloat16, jnp.float32
    own, width = tokens.shape
    group_rows, top = expert_ids.shape
    experts, _, hidden = w_gate.shape
    ring = lax.axis_size("dp")
    step = split_at(width, 512)
    chunks = width // step
    cut = split_at(step, 256)
    cuts = width // cut
    token_half = ring * 4 * own
    anywhere = pl.BlockSpec(memory_space=pl.ANY)
    in_vmem = pl.BlockSpec(memory_space=pltpu.VMEM)
    shape = lambda *dims: jax.ShapeDtypeStruct(dims, bf16)
    dma = lambda *dims: pltpu.SemaphoreType.DMA(dims)
    matmul = 2 * experts * row_count * width * hidden
    return pl.pallas_call(
        layer_kernel,
        in_specs=[anywhere, anywhere, in_vmem, in_vmem, anywhere, anywhere, anywhere],
        out_specs=[anywhere] * 4 + [in_vmem] * 2,
        out_shape=[
            shape(experts, row_count, width),
            shape(experts, row_count, width),
            shape(experts, row_count, hidden),
            shape(experts, row_count, 2 * hidden),
            shape(own, width),
            shape(own, width),
        ],
        scratch_shapes=[
            pltpu.VMEM((chunks, 2, ring, 2, 2, 2, own, step), bf16),
            pltpu.VMEM((ring, 2, group_rows, 128), bf16),
            pltpu.VMEM((experts, width, 2 * hidden), bf16),
            pltpu.VMEM((experts, hidden, width), bf16),
            pltpu.VMEM((2, 2, experts, row_count, step), bf16),
            pltpu.VMEM((experts, row_count, 2 * hidden), f32),
            pltpu.VMEM((experts, row_count, hidden), f32),
            pltpu.VMEM((experts, row_count, hidden), bf16),
            pltpu.VMEM((experts, row_count, 2 * hidden), bf16),
            pltpu.VMEM((2, experts * row_count // 2, token_half), bf16),
            pltpu.VMEM((2, token_half, experts * row_count // 2), bf16),
            pltpu.VMEM((experts, row_count, 128), f32),
            pltpu.VMEM((cuts, 2, ring, 2, 2, own, cut), bf16),
            pltpu.VMEM((cuts, 2, ring, 2, own, cut), bf16),
            pltpu.VMEM((cuts, 2, ring, own, cut), bf16),
            pltpu.VMEM((cuts, 2, ring - 1, own, cut), bf16),
            dma(chunks, 2), dma(chunks, 3), dma(2, 2), dma(2),
            dma(ring), dma(ring), dma(chunks, 2, ring), dma(chunks, 2, ring),
            dma(2, 3), dma(2, 3), dma(chunks, 2, 3), dma(chunks, 2, 3),
            dma(cuts, 2, ring + 2), dma(cuts, 2, ring + 2),
        ],
        compiler_params=pltpu.CompilerParams(
            collective_id=0, has_side_effects=True, vmem_limit_bytes=63 << 20
        ),
        cost_estimate=pl.CostEstimate(
            flops=6 * matmul, bytes_accessed=6 * experts * width * hidden, transcendentals=0
        ),
        name="layer",
    )(tokens, grad_out, expert_ids, router_weights, w_gate, w_up, w_down)


def weights_kernel(inputs, cotangent, act, pre, layer, grad, gate_out, up_out, down_out, layer_out, grad_out):
    f32, bf16 = jnp.float32, jnp.bfloat16
    hidden = act.shape[2]

    @pl.when(pl.program_id(0) == 0)
    def _():
        layer_out[...] = layer[...]
        grad_out[...] = grad[...]

    gate_out[0] = lax.dot_general(
        inputs[0], pre[0, :, 0:hidden], contract_first, preferred_element_type=f32
    ).astype(bf16)
    up_out[0] = lax.dot_general(
        inputs[0], pre[0, :, hidden : 2 * hidden], contract_first, preferred_element_type=f32
    ).astype(bf16)
    down_out[0] = lax.dot_general(
        act[0], cotangent[0], contract_first, preferred_element_type=f32
    ).astype(bf16)


def gathered_shards(tokens, grad_out, expert_ids, router_weights, w_gate, w_up, w_down):
    bf16 = jnp.bfloat16
    own, width = tokens.shape
    group_rows, top_count = expert_ids.shape
    experts, _, hidden = w_gate.shape
    groups = lax.axis_size(("dp", "ctx"))
    row_count = groups * (2 * group_rows * top_count // (groups * experts))
    inputs, cotangent, act, pre, layer, grad = run_layer(
        tokens, grad_out, expert_ids, router_weights, w_gate, w_up, w_down, row_count
    )
    whole = lambda *shape: pl.BlockSpec(shape, lambda e: (0,) * len(shape))
    each = lambda *shape: pl.BlockSpec((1, *shape), lambda e: (e, 0, 0))
    matmul = 2 * experts * row_count * width * hidden
    grad_gate, grad_up, grad_down, layer, grad = pl.pallas_call(
        weights_kernel,
        grid=(experts,),
        in_specs=[
            each(row_count, width),
            each(row_count, width),
            each(row_count, hidden),
            each(row_count, 2 * hidden),
            whole(own, width),
            whole(own, width),
        ],
        out_specs=[
            each(width, hidden), each(width, hidden), each(hidden, width),
            whole(own, width), whole(own, width),
        ],
        out_shape=[
            jax.ShapeDtypeStruct(w_gate.shape, bf16),
            jax.ShapeDtypeStruct(w_up.shape, bf16),
            jax.ShapeDtypeStruct(w_down.shape, bf16),
            jax.ShapeDtypeStruct(tokens.shape, bf16),
            jax.ShapeDtypeStruct(tokens.shape, bf16),
        ],
        compiler_params=pltpu.CompilerParams(vmem_limit_bytes=60 << 20),
        cost_estimate=pl.CostEstimate(
            flops=3 * matmul, bytes_accessed=6 * experts * width * hidden, transcendentals=0
        ),
        name="expert_weights",
    )(inputs, cotangent, act, pre, layer, grad)
    return layer, grad, grad_gate, grad_up, grad_down


def solution(mesh):
    def per_device(tokens, *rest):
        devices = lax.axis_size(("dp", "ctx", "tp"))
        few = tokens.shape[0] * devices <= 1024
        few = few and lax.axis_size("ctx") == 2 and lax.axis_size("tp") == 4
        return (gathered_shards if few else shards)(tokens, *rest)

    placed = (
        P(("dp", "ctx", "tp"), None),
        P(("dp", "ctx", "tp"), None),
        P(("dp", "ctx"), None),
        P(("dp", "ctx"), None),
        P(("dp", "ctx"), None, "tp"),
        P(("dp", "ctx"), None, "tp"),
        P(("dp", "ctx"), "tp", None),
    )
    return jax.shard_map(
        per_device,
        mesh=mesh,
        in_specs=placed,
        out_specs=(
            P(("dp", "ctx", "tp"), None),
            P(("dp", "ctx", "tp"), None),
            P(("dp", "ctx"), None, "tp"),
            P(("dp", "ctx"), None, "tp"),
            P(("dp", "ctx"), "tp", None),
        ),
        check_vma=False,
    )
```

```python
import jax
import jax.numpy as jnp
from jax import lax
from jax.experimental import pallas as pl
from jax.experimental.pallas import tpu as pltpu
from jax.sharding import PartitionSpec as P

contract_last = (((1,), (1,)), ((), ()))
contract_first = (((0,), (0,)), ((), ()))


def swiglu_rows(inputs, cotangent, row_weights, gate_w, up_w, down_w):
    gate = jnp.dot(inputs, gate_w, preferred_element_type=jnp.float32)
    upward = jnp.dot(inputs, up_w, preferred_element_type=jnp.float32)
    sigmoid_gate = jax.nn.sigmoid(gate)
    row_scale = row_weights.astype(jnp.float32)[:, None]
    activation = (row_scale * gate * sigmoid_gate * upward).astype(jnp.bfloat16)
    output_rows = jnp.dot(activation, down_w, preferred_element_type=jnp.float32).astype(
        jnp.bfloat16
    )
    backward = lax.dot_general(cotangent, down_w, contract_last, preferred_element_type=jnp.float32)
    grad_gate_pre = (
        backward * row_scale * upward * sigmoid_gate * (1.0 + gate * (1.0 - sigmoid_gate))
    ).astype(jnp.bfloat16)
    grad_up_pre = (backward * row_scale * gate * sigmoid_gate).astype(jnp.bfloat16)
    input_rows = (
        lax.dot_general(grad_gate_pre, gate_w, contract_last, preferred_element_type=jnp.float32)
        + lax.dot_general(grad_up_pre, up_w, contract_last, preferred_element_type=jnp.float32)
    ).astype(jnp.bfloat16)
    grad_down = lax.dot_general(
        activation, cotangent, contract_first, preferred_element_type=jnp.float32
    )
    grad_gate = lax.dot_general(
        inputs, grad_gate_pre, contract_first, preferred_element_type=jnp.float32
    )
    grad_up = lax.dot_general(
        inputs, grad_up_pre, contract_first, preferred_element_type=jnp.float32
    )
    return (output_rows, input_rows, grad_gate, grad_up, grad_down)


def shards(tokens, grad_out, expert_ids, router_weights, w_gate, w_up, w_down):
    expert_devices = lax.axis_size(("dp", "ctx"))
    group_rows, top_count = expert_ids.shape
    local_experts = w_gate.shape[0]
    expert_total = expert_devices * local_experts
    slot_most = 2 * group_rows * top_count // expert_total
    model_width = tokens.shape[1]
    group_tokens, group_grads = (
        lax.all_to_all(tokens, "tp", split_axis=1, concat_axis=0, tiled=True),
        lax.all_to_all(grad_out, "tp", split_axis=1, concat_axis=0, tiled=True),
    )
    carried = group_tokens.shape[1]
    flat_ids = expert_ids.reshape(-1)
    onehot = (flat_ids[:, None] == jnp.arange(expert_total, dtype=jnp.int32)[None, :]).astype(
        jnp.int32
    )
    place = jnp.arange(flat_ids.shape[0], dtype=jnp.int32)
    before = (place[:, None] > place[None, :]).astype(jnp.bfloat16)
    earlier = jnp.dot(
        before, onehot.astype(jnp.bfloat16), preferred_element_type=jnp.float32
    ).astype(jnp.int32)
    ranks = jnp.sum(earlier * onehot, axis=1)
    slots = flat_ids * slot_most + ranks
    assignments = group_rows * top_count
    source = (
        jnp.full((expert_total * slot_most,), assignments, jnp.int32)
        .at[slots]
        .set(jnp.arange(assignments, dtype=jnp.int32))
    )
    token_of = source // top_count
    zero_row = jnp.zeros((1, carried), jnp.bfloat16)
    send_tokens = jnp.concatenate([group_tokens, zero_row], axis=0)[token_of].reshape(
        expert_devices, local_experts * slot_most, carried
    )
    send_grads = jnp.concatenate([group_grads, zero_row], axis=0)[token_of].reshape(
        expert_devices, local_experts * slot_most, carried
    )
    send_weights = jnp.concatenate(
        [router_weights.reshape(-1), jnp.zeros((1,), jnp.bfloat16)], axis=0
    )[source].reshape(expert_devices, local_experts * slot_most)
    recv_tokens, recv_grads, recv_weights = (
        lax.all_to_all(send_tokens, ("dp", "ctx"), split_axis=0, concat_axis=0, tiled=True),
        lax.all_to_all(send_grads, ("dp", "ctx"), split_axis=0, concat_axis=0, tiled=True),
        lax.all_to_all(send_weights, ("dp", "ctx"), split_axis=0, concat_axis=0, tiled=True),
    )
    recv_tokens, recv_grads = (
        lax.all_gather(recv_tokens, "tp", axis=2, tiled=True),
        lax.all_gather(recv_grads, "tp", axis=2, tiled=True),
    )
    token_grid = recv_tokens.reshape(expert_devices, local_experts, slot_most, model_width)
    grad_grid = recv_grads.reshape(expert_devices, local_experts, slot_most, model_width)
    weight_grid = recv_weights.reshape(expert_devices, local_experts, slot_most)
    outputs = []
    for expert_index in range(local_experts):
        outputs.append(
            swiglu_rows(
                token_grid[:, expert_index].reshape(-1, model_width),
                grad_grid[:, expert_index].reshape(-1, model_width),
                weight_grid[:, expert_index].reshape(-1),
                w_gate[expert_index],
                w_up[expert_index],
                w_down[expert_index],
            )
        )
    out_rows = jnp.stack(
        [entry[0].reshape(expert_devices, slot_most, model_width) for entry in outputs], axis=1
    ).reshape(expert_devices, local_experts * slot_most, model_width)
    in_rows = jnp.stack(
        [entry[1].reshape(expert_devices, slot_most, model_width) for entry in outputs], axis=1
    ).reshape(expert_devices, local_experts * slot_most, model_width)
    grad_gate = jnp.stack([entry[2] for entry in outputs], axis=0).astype(jnp.bfloat16)
    grad_up = jnp.stack([entry[3] for entry in outputs], axis=0).astype(jnp.bfloat16)
    grad_down = jnp.stack([entry[4] for entry in outputs], axis=0).astype(jnp.bfloat16)
    slot_grid = slots.reshape(group_rows, top_count)

    def combine(table):
        picked = table.reshape(expert_total * slot_most, -1)[slot_grid]
        return jnp.sum(picked, axis=1)

    column_out, column_in = (
        lax.psum_scatter(
            out_rows.astype(jnp.float32).astype(jnp.bfloat16), "tp", scatter_dimension=2, tiled=True
        ).astype(jnp.float32),
        lax.psum_scatter(
            in_rows.astype(jnp.float32).astype(jnp.bfloat16), "tp", scatter_dimension=2, tiled=True
        ).astype(jnp.float32),
    )
    back_out, back_in = (
        lax.all_to_all(
            column_out.astype(jnp.bfloat16), ("dp", "ctx"), split_axis=0, concat_axis=0, tiled=True
        ).astype(column_out.dtype),
        lax.all_to_all(
            column_in.astype(jnp.bfloat16), ("dp", "ctx"), split_axis=0, concat_axis=0, tiled=True
        ).astype(column_in.dtype),
    )
    layer_out, grad_tokens = (
        lax.all_to_all(
            combine(back_out).astype(jnp.bfloat16), "tp", split_axis=0, concat_axis=1, tiled=True
        ).astype(jnp.float32),
        lax.all_to_all(
            combine(back_in).astype(jnp.bfloat16), "tp", split_axis=0, concat_axis=1, tiled=True
        ).astype(jnp.float32),
    )
    return (
        layer_out.astype(jnp.bfloat16),
        grad_tokens.astype(jnp.bfloat16),
        grad_gate,
        grad_up,
        grad_down,
    )


def split_at(total, most):
    size = most
    while total % size:
        size //= 2
    return size


class Place:
    def __init__(self):
        self.ring = lax.axis_size("dp")
        self.z, self.x = lax.axis_index("dp"), lax.axis_index("ctx")
        tp = lax.axis_index("tp")
        self.y, self.c = tp // 2, tp % 2

    def device(self, z=None, x=None, y=None, c=None):
        pick = lambda value, own: own if value is None else value
        tp = pick(y, self.y) * 2 + pick(c, self.c)
        return (pick(z, self.z), pick(x, self.x), tp)

    def ahead(self, k):
        return self.device(z=lax.rem(self.z + k, self.ring))

    def core_peer(self):
        return self.device(c=1 - self.c)

    def x_peer(self):
        return self.device(x=1 - self.x)

    def y_peer(self):
        return self.device(y=1 - self.y)

    def greet(self):
        barrier = pltpu.get_barrier_semaphore()
        others = [self.core_peer(), self.x_peer(), self.y_peer()]
        others += [self.ahead(k) for k in range(1, self.ring)]
        for other in others:
            pl.semaphore_signal(
                barrier, inc=1, device_id=other, device_id_type=pl.DeviceIdType.MESH
            )
        return lambda: pl.semaphore_wait(barrier, len(others))


gather_order = [
    ("along", 0, 1), ("along", 0, 0), ("along", 1, 0), ("along", 2, 1), ("along", 2, 0),
    ("along", 3, 1), ("own0", 0, 0), ("along", 3, 0), ("along", 1, 1), ("own0", 0, 1),
    ("enter", 0, 1), ("enter", 0, 0), ("routes", 0, 0), ("own1", 0, 0), ("own1", 0, 1), ("route", 0, 0),
    ("enter", 2, 1), ("enter", 1, 0), ("across", 0, 0), ("across", 0, 1), ("enter", 2, 0),
    ("own2", 0, 0), ("enter", 3, 1), ("own2", 0, 1), ("across", 2, 1), ("across", 1, 0),
    ("enter", 3, 0), ("core", 0, 0), ("enter", 1, 1), ("core", 0, 1), ("across", 3, 1),
    ("across", 2, 0), ("work", 0, 0), ("core", 1, 0), ("work", 0, 1), ("across", 1, 1),
    ("across", 3, 0), ("core", 2, 1), ("work", 1, 0), ("core", 2, 0), ("work", 2, 1),
    ("core", 3, 1), ("work", 2, 0), ("core", 3, 0), ("core", 1, 1), ("work", 3, 1), ("work", 3, 0),
    ("work", 1, 1),
]

reduce_order = [
    ("products", 0, 0), ("products", 0, 1), ("fold0", 0, 0), ("products", 1, 0),
    ("products", 1, 1), ("fold0", 0, 1), ("fold0", 1, 0), ("products", 2, 0), ("fold1", 0, 0),
    ("fold0", 1, 1), ("products", 2, 1), ("fold0", 2, 0), ("fold1", 0, 1), ("fold1", 1, 0),
    ("products", 3, 0), ("fold0", 2, 1), ("fold2", 0, 0), ("products", 3, 1), ("fold0", 3, 0),
    ("products", 4, 0), ("fold1", 1, 1), ("products", 4, 1), ("fold1", 2, 0), ("fold2", 0, 1),
    ("finish", 0, 0), ("fold0", 4, 0), ("fold0", 3, 1), ("fold2", 1, 0), ("fold0", 4, 1),
    ("fold1", 3, 0), ("fold1", 2, 1), ("fold2", 1, 1), ("fold2", 2, 0), ("finish", 0, 1),
    ("fold1", 4, 0), ("fold1", 3, 1), ("finish", 1, 0), ("fold2", 2, 1), ("fold1", 4, 1),
    ("finish", 1, 1), ("fold2", 3, 0), ("fold2", 4, 0), ("fold2", 3, 1), ("finish", 2, 0),
    ("fold2", 4, 1), ("finish", 2, 1), ("finish", 3, 0), ("finish", 4, 0), ("finish", 3, 1),
    ("finish", 4, 1),
]

reduce_pieces = [(0, 512), (512, 512), (1024, 512), (1536, 256), (1792, 256)]


def layer_kernel(
    tok, grd, ids, weights, gate_w, up_w, down_w,
    inputs_out, cotangent_out, act_out, pre_out, layer_out, grad_out,
    tab, routes, wide, down, rows, wide_acc, back_acc, act, pre, pick, place, scale,
    got1, got2, got3, got4,
    own_sem, weight_sem, row_sem, hidden_sem,
    route_send, route_recv, along_send, along_recv, own_send, own_recv, part_send, part_recv,
    red_send, red_recv,
):
    f32, bf16, i32 = jnp.float32, jnp.bfloat16, jnp.int32
    at = Place()
    x, y, c, ring = at.x, at.y, at.c, at.ring
    chunks, step = tab.shape[0], tab.shape[-1]
    own_count = tab.shape[-2]
    experts, hidden, width = down.shape
    half_rows = rows.shape[3] // 2
    token_half = pick.shape[2]
    half_ring = ring // 2
    all_rows = experts * half_rows
    top, group_rows = ids.shape
    cols = lambda n, size: pl.ds(n * size, size)

    def send(source, target, send_sem, recv_sem, device):
        copy = pltpu.make_async_remote_copy(
            src_ref=source, dst_ref=target, send_sem=send_sem, recv_sem=recv_sem,
            device_id=device, device_id_type=pl.DeviceIdType.MESH,
        )
        copy.start()
        return copy

    def local(source, target, sem):
        copy = pltpu.make_async_copy(source, target, sem)
        copy.start()
        return copy

    met = at.greet()
    own_loads = [
        local(table.at[:, cols(n, step)], tab.at[n, h, 0, x, y, c], own_sem.at[n, h])
        for n in range(chunks)
        for h, table in enumerate((tok, grd))
    ]
    weight_loads = [
        (
            local(gate_w.at[:, cols(n, step)], wide.at[:, cols(n, step), pl.ds(0, hidden)],
                  weight_sem.at[n, 0]),
            local(up_w.at[:, cols(n, step)], wide.at[:, cols(n, step), pl.ds(hidden, hidden)],
                  weight_sem.at[n, 1]),
            local(down_w.at[:, :, cols(n, step)], down.at[:, :, cols(n, step)],
                  weight_sem.at[n, 2]),
        )
        for n in range(chunks)
    ]
    own_route = jnp.concatenate([ids[...].astype(f32), weights[...].astype(f32)], axis=0)
    routes[0, x] = jnp.concatenate(
        [own_route, jnp.zeros((2 * top, routes.shape[3] - group_rows), f32)], axis=1
    ).astype(bf16)
    for copy in own_loads:
        copy.wait()
    met()

    route_along = [
        send(routes.at[0, x], routes.at[ring - k, x], route_send.at[k], route_recv.at[k],
             at.ahead(k))
        for k in range(1, ring)
    ]
    peers = ((at.x_peer(), at.y_peer()), (at.y_peer(), at.x_peer()))

    def stage_ref(lead, h, stage):
        if stage == 0:
            return tab.at[(*lead, x, y, c)]
        if stage == 1:
            return tab.at[(*lead, slice(None), y, c)] if h == 0 else tab.at[(*lead, x, slice(None), c)]
        return tab.at[(*lead, slice(None), slice(None), c)]

    owns, along, parts, across, row_saves = {}, {}, {}, [], {}

    def own_stage(h, stage):
        if stage:
            owns[h, stage - 1].wait_recv()
        ref = stage_ref((slice(None), h, 0), h, stage)
        peer = at.core_peer() if stage == 2 else peers[h][stage]
        owns[h, stage] = send(ref, ref, own_send.at[h, stage], own_recv.at[h, stage], peer)

    def send_along(n, h):
        for k in range(1, ring):
            along[n, h, k] = send(
                tab.at[n, h, 0, x, y, c], tab.at[n, h, ring - k, x, y, c],
                along_send.at[n, h, k], along_recv.at[n, h, k], at.ahead(k),
            )

    def part_stage(n, h, stage):
        if stage:
            parts[n, h, stage - 1].wait_recv()
        else:
            for k in range(1, ring):
                along[n, h, k].wait_recv()
        ref = stage_ref((n, h, pl.ds(1, ring - 1)), h, stage)
        peer = at.core_peer() if stage == 2 else peers[h][stage]
        parts[n, h, stage] = send(
            ref, ref, part_send.at[n, h, stage], part_recv.at[n, h, stage], peer
        )

    def send_routes():
        for copy in route_along:
            copy.wait_recv()
        across.append(
            send(routes.at[:, x], routes.at[:, x], route_send.at[0], route_recv.at[0], at.x_peer())
        )

    def find_rows():
        across[0].wait_recv()
        first = (lax.axis_index(("dp", "ctx")) * experts).astype(f32)
        blocks = [
            routes[k, side].astype(f32)[:, 0:group_rows] for k in range(ring) for side in range(2)
        ]
        table = jnp.concatenate(blocks, axis=1)
        named_ids, named_weights = table[0:top], table[top : 2 * top]
        hits, scales = [], []
        for e in range(experts):
            named = named_ids == first + e
            hits.append(jnp.max(jnp.where(named, 1.0, 0.0), axis=0, keepdims=True))
            scales.append(jnp.sum(jnp.where(named, named_weights, 0.0), axis=0, keepdims=True))
        before = jnp.where(
            lax.broadcasted_iota(i32, (token_half, token_half), 0)
            < lax.broadcasted_iota(i32, (token_half, token_half), 1),
            1.0, 0.0,
        ).astype(bf16)
        hit_all = jnp.concatenate(hits, axis=0)
        spots = lax.broadcasted_iota(i32, (half_rows, token_half), 0).astype(f32)
        lanes = lax.broadcasted_iota(i32, (token_half, 2 * half_rows), 1).astype(f32)
        for half in range(2):
            here = slice(half * token_half, (half + 1) * token_half)
            hit = hit_all[:, here]
            rank = jnp.dot(hit.astype(bf16), before, preferred_element_type=f32)
            order = jnp.where(hit > 0.5, rank, -256.0)
            order_col = order.T
            for e in range(experts):
                chosen = spots == order[e : e + 1]
                pick[half, e * half_rows : (e + 1) * half_rows] = jnp.where(
                    chosen, 1.0, 0.0
                ).astype(bf16)
                scale[e, half * half_rows : (half + 1) * half_rows] = jnp.broadcast_to(
                    jnp.sum(jnp.where(chosen, scales[e][:, here], 0.0), axis=1, keepdims=True),
                    (half_rows, scale.shape[2]),
                )
            for e in range(0, experts, 2):
                spot = jnp.where(
                    lanes < half_rows, order_col[:, e : e + 1], order_col[:, e + 1 : e + 2] + half_rows
                )
                place[half, :, e * half_rows : (e + 2) * half_rows] = jnp.where(
                    spot == lanes, 1.0, 0.0
                ).astype(bf16)

    def work(n, h):
        if (n, h) == (0, 0):
            for side in range(2):
                owns[side, 2].wait_recv()
        parts[n, h, 2].wait_recv()
        for copy in weight_loads[n][0:2] if h == 0 else weight_loads[n][2:3]:
            copy.wait()
        slot = n % 2
        if (slot, h) in row_saves:
            row_saves[slot, h].wait()
        for half in range(2):
            block = tab[n, h, half * half_ring : (half + 1) * half_ring].reshape(token_half, step)
            picked = jnp.dot(pick[half], block, preferred_element_type=f32).astype(bf16)
            rows[slot, h, :, half * half_rows : (half + 1) * half_rows] = picked.reshape(
                experts, half_rows, step
            )
        out = inputs_out if h == 0 else cotangent_out
        row_saves[slot, h] = local(
            rows.at[slot, h], out.at[:, :, cols(n, step)], row_sem.at[slot, h]
        )
        fresh = (h not in started)
        started.add(h)

        @pl.loop(0, experts, unroll=experts)
        def _(e):
            if h == 0:
                value = jnp.dot(rows[slot, h, e], wide[e, n * step : (n + 1) * step],
                                preferred_element_type=f32)
                wide_acc[e] = value if fresh else wide_acc[e] + value
            else:
                value = lax.dot_general(
                    rows[slot, h, e], down[e, :, n * step : (n + 1) * step], contract_last,
                    preferred_element_type=f32,
                )
                back_acc[e] = value if fresh else back_acc[e] + value

    started = set()
    doing = {
        "own0": lambda n, h: own_stage(h, 0),
        "own1": lambda n, h: own_stage(h, 1),
        "own2": lambda n, h: own_stage(h, 2),
        "along": send_along,
        "enter": lambda n, h: part_stage(n, h, 0),
        "across": lambda n, h: part_stage(n, h, 1),
        "core": lambda n, h: part_stage(n, h, 2),
        "routes": lambda n, h: send_routes(),
        "route": lambda n, h: find_rows(),
        "work": work,
    }
    for name, n, h in gather_order:
        doing[name](n, h)

    @pl.loop(0, experts)
    def _(e):
        gate = wide_acc[e, :, 0:hidden]
        upward = wide_acc[e, :, hidden : 2 * hidden]
        backward = back_acc[e]
        row_scale = scale[e][:, 0:1]
        sigmoid_gate = jax.nn.sigmoid(gate)
        silu = row_scale * gate * sigmoid_gate
        act[e] = (silu * upward).astype(bf16)
        pre[e, :, 0:hidden] = (
            backward * row_scale * upward * sigmoid_gate * (1.0 + gate * (1.0 - sigmoid_gate))
        ).astype(bf16)
        pre[e, :, hidden : 2 * hidden] = (backward * silu).astype(bf16)

    hidden_saves = [local(act, act_out, hidden_sem.at[0]), local(pre, pre_out, hidden_sem.at[1])]
    for copy in row_saves.values():
        copy.wait()
    for copies in (route_along, across, owns.values(), along.values(), parts.values()):
        for copy in copies:
            copy.wait_send()

    red = {}
    back_peers = ((at.y_peer(), at.x_peer()), (at.x_peer(), at.y_peer()))

    def reduce_send(d, h, stage, source, target, device):
        red[d, h, stage] = send(
            source, target, red_send.at[d, h, stage], red_recv.at[d, h, stage], device
        )

    def piece(d):
        start, size = reduce_pieces[d]
        return start // step, pl.ds(start % step, size), start, size

    def products(d, h):
        n, lanes, start, size = piece(d)
        slot = d % 2

        @pl.loop(0, experts, unroll=experts)
        def _(e):
            if h == 0:
                value = jnp.dot(act[e], down[e, :, start : start + size],
                                preferred_element_type=f32)
            else:
                value = lax.dot_general(
                    pre[e], wide[e, start : start + size], contract_last,
                    preferred_element_type=f32,
                )
            rows[slot, h, e, :, 0:size] = value.astype(bf16)

        for half in range(2):
            block = rows[slot, h, :, half * half_rows : (half + 1) * half_rows, 0:size].reshape(
                all_rows, size
            )
            value = jnp.dot(place[half], block, preferred_element_type=f32).astype(bf16)
            tab[n, h, half * half_ring : (half + 1) * half_ring, :, :, :, :, lanes] = value.reshape(
                half_ring, 2, 2, 2, own_count, size
            )
        reduce_send(d, h, 0, tab.at[n, h, :, :, :, 1 - c, :, lanes],
                    got1.at[n, h, :, :, :, :, lanes], at.core_peer())

    def fold_core(d, h):
        n, lanes, _, _ = piece(d)
        red[d, h, 0].wait_recv()
        tab[n, h, :, :, :, c, :, lanes] = (
            tab[n, h, :, :, :, c, :, lanes].astype(f32) + got1[n, h, :, :, :, :, lanes].astype(f32)
        ).astype(bf16)
        part = (
            tab.at[n, h, :, :, 1 - y, c, :, lanes] if h == 0 else tab.at[n, h, :, 1 - x, :, c, :, lanes]
        )
        reduce_send(d, h, 1, part, got2.at[n, h, :, :, :, lanes], back_peers[h][0])

    def fold_first(d, h):
        n, lanes, _, _ = piece(d)
        red[d, h, 1].wait_recv()
        mine = (n, h, slice(None), slice(None), y, c) if h == 0 else (n, h, slice(None), x, slice(None), c)
        tab[(*mine, slice(None), lanes)] = (
            tab[(*mine, slice(None), lanes)].astype(f32) + got2[n, h, :, :, :, lanes].astype(f32)
        ).astype(bf16)
        part = (
            tab.at[n, h, :, 1 - x, y, c, :, lanes] if h == 0 else tab.at[n, h, :, x, 1 - y, c, :, lanes]
        )
        reduce_send(d, h, 2, part, got3.at[n, h, :, :, lanes], back_peers[h][1])

    def fold_second(d, h):
        n, lanes, _, _ = piece(d)
        red[d, h, 2].wait_recv()
        tab[n, h, :, x, y, c, :, lanes] = (
            tab[n, h, :, x, y, c, :, lanes].astype(f32) + got3[n, h, :, :, lanes].astype(f32)
        ).astype(bf16)
        for k in range(1, ring):
            reduce_send(
                d, h, 2 + k, tab.at[n, h, k, x, y, c, :, lanes], got4.at[n, h, k - 1, :, lanes],
                at.ahead(k),
            )

    def finish(d, h):
        n, lanes, start, size = piece(d)
        total = tab[n, h, 0, x, y, c, :, lanes].astype(f32)
        for k in range(1, ring):
            red[d, h, 2 + k].wait_recv()
            total = total + got4[n, h, k - 1, :, lanes].astype(f32)
        out = layer_out if h == 0 else grad_out
        out[:, start : start + size] = total.astype(bf16)

    doing = {
        "products": products, "fold0": fold_core, "fold1": fold_first, "fold2": fold_second,
        "finish": finish,
    }
    for name, d, h in reduce_order:
        doing[name](d, h)
    for copy in red.values():
        copy.wait_send()
    for copy in hidden_saves:
        copy.wait()


def run_layer(tokens, grad_out, expert_ids, router_weights, w_gate, w_up, w_down, row_count):
    bf16, f32 = jnp.bfloat16, jnp.float32
    own, width = tokens.shape
    group_rows, top = expert_ids.shape
    experts, _, hidden = w_gate.shape
    ring = lax.axis_size("dp")
    step = split_at(width, 512)
    chunks = width // step
    cuts = len(reduce_pieces)
    token_half = ring * 4 * own
    anywhere = pl.BlockSpec(memory_space=pl.ANY)
    in_vmem = pl.BlockSpec(memory_space=pltpu.VMEM)
    shape = lambda *dims: jax.ShapeDtypeStruct(dims, bf16)
    dma = lambda *dims: pltpu.SemaphoreType.DMA(dims)
    matmul = 2 * experts * row_count * width * hidden
    return pl.pallas_call(
        layer_kernel,
        in_specs=[anywhere, anywhere, in_vmem, in_vmem, anywhere, anywhere, anywhere],
        out_specs=[anywhere] * 4 + [in_vmem] * 2,
        out_shape=[
            shape(experts, row_count, width),
            shape(experts, row_count, width),
            shape(experts, row_count, hidden),
            shape(experts, row_count, 2 * hidden),
            shape(own, width),
            shape(own, width),
        ],
        scratch_shapes=[
            pltpu.VMEM((chunks, 2, ring, 2, 2, 2, own, step), bf16),
            pltpu.VMEM((ring, 2, 2 * top, 128), bf16),
            pltpu.VMEM((experts, width, 2 * hidden), bf16),
            pltpu.VMEM((experts, hidden, width), bf16),
            pltpu.VMEM((2, 2, experts, row_count, step), bf16),
            pltpu.VMEM((experts, row_count, 2 * hidden), f32),
            pltpu.VMEM((experts, row_count, hidden), f32),
            pltpu.VMEM((experts, row_count, hidden), bf16),
            pltpu.VMEM((experts, row_count, 2 * hidden), bf16),
            pltpu.VMEM((2, experts * row_count // 2, token_half), bf16),
            pltpu.VMEM((2, token_half, experts * row_count // 2), bf16),
            pltpu.VMEM((experts, row_count, 128), f32),
            pltpu.VMEM((chunks, 2, ring, 2, 2, own, step), bf16),
            pltpu.VMEM((chunks, 2, ring, 2, own, step), bf16),
            pltpu.VMEM((chunks, 2, ring, own, step), bf16),
            pltpu.VMEM((chunks, 2, ring - 1, own, step), bf16),
            dma(chunks, 2), dma(chunks, 3), dma(2, 2), dma(2),
            dma(ring), dma(ring), dma(chunks, 2, ring), dma(chunks, 2, ring),
            dma(2, 3), dma(2, 3), dma(chunks, 2, 3), dma(chunks, 2, 3),
            dma(cuts, 2, ring + 2), dma(cuts, 2, ring + 2),
        ],
        compiler_params=pltpu.CompilerParams(
            collective_id=0, has_side_effects=True, vmem_limit_bytes=63 << 20
        ),
        cost_estimate=pl.CostEstimate(
            flops=6 * matmul, bytes_accessed=6 * experts * width * hidden, transcendentals=0
        ),
        name="layer",
    )(tokens, grad_out, expert_ids.T, router_weights.T, w_gate, w_up, w_down)


def weights_kernel(
    inputs, cotangent, act, pre, layer, grad, gate_out, up_out, down_out, layer_out, grad_out,
    inputs_all, cotangent_all, act_all, pre_all, gate_part, up_part, down_part, in_sem, out_sem,
):
    f32, bf16 = jnp.float32, jnp.bfloat16
    experts, _, hidden = act.shape
    slots = gate_part.shape[0]

    def copy(source, target, sem):
        moved = pltpu.make_async_copy(source, target, sem)
        moved.start()
        return moved

    tables = ((inputs, inputs_all), (pre, pre_all), (act, act_all), (cotangent, cotangent_all))
    loads = [
        [
            copy(source.at[e], target.at[e], in_sem.at[e, k])
            for k, (source, target) in enumerate(tables)
        ]
        for e in range(experts)
    ]
    layer_out[...] = layer[...]
    grad_out[...] = grad[...]
    saves = {}

    def product(k, e, part, out, rows, columns):
        slot = e % slots
        if e >= slots:
            saves[k, e - slots].wait()
        part[slot] = lax.dot_general(
            rows, columns, contract_first, preferred_element_type=f32
        ).astype(bf16)
        saves[k, e] = copy(part.at[slot], out.at[e], out_sem.at[slot, k])

    for e in range(experts):
        loads[e][0].wait()
        loads[e][1].wait()
        product(0, e, gate_part, gate_out, inputs_all[e], pre_all[e, :, 0:hidden])
        product(1, e, up_part, up_out, inputs_all[e], pre_all[e, :, hidden : 2 * hidden])
        loads[e][2].wait()
        loads[e][3].wait()
        product(2, e, down_part, down_out, act_all[e], cotangent_all[e])
    for e in range(max(0, experts - slots), experts):
        for k in range(3):
            saves[k, e].wait()


def gathered_shards(tokens, grad_out, expert_ids, router_weights, w_gate, w_up, w_down):
    bf16 = jnp.bfloat16
    own, width = tokens.shape
    group_rows, top_count = expert_ids.shape
    experts, _, hidden = w_gate.shape
    groups = lax.axis_size(("dp", "ctx"))
    row_count = groups * (2 * group_rows * top_count // (groups * experts))
    inputs, cotangent, act, pre, layer, grad = run_layer(
        tokens, grad_out, expert_ids, router_weights, w_gate, w_up, w_down, row_count
    )
    anywhere = pl.BlockSpec(memory_space=pl.ANY)
    in_vmem = pl.BlockSpec(memory_space=pltpu.VMEM)
    matmul = 2 * experts * row_count * width * hidden
    slots = min(3, experts)
    grad_gate, grad_up, grad_down, layer, grad = pl.pallas_call(
        weights_kernel,
        in_specs=[anywhere] * 4 + [in_vmem] * 2,
        out_specs=[anywhere] * 3 + [in_vmem] * 2,
        out_shape=[
            jax.ShapeDtypeStruct(w_gate.shape, bf16),
            jax.ShapeDtypeStruct(w_up.shape, bf16),
            jax.ShapeDtypeStruct(w_down.shape, bf16),
            jax.ShapeDtypeStruct(tokens.shape, bf16),
            jax.ShapeDtypeStruct(tokens.shape, bf16),
        ],
        scratch_shapes=[
            pltpu.VMEM((experts, row_count, width), bf16),
            pltpu.VMEM((experts, row_count, width), bf16),
            pltpu.VMEM((experts, row_count, hidden), bf16),
            pltpu.VMEM((experts, row_count, 2 * hidden), bf16),
            pltpu.VMEM((slots, width, hidden), bf16),
            pltpu.VMEM((slots, width, hidden), bf16),
            pltpu.VMEM((slots, hidden, width), bf16),
            pltpu.SemaphoreType.DMA((experts, 4)),
            pltpu.SemaphoreType.DMA((slots, 3)),
        ],
        compiler_params=pltpu.CompilerParams(vmem_limit_bytes=60 << 20),
        cost_estimate=pl.CostEstimate(
            flops=3 * matmul, bytes_accessed=6 * experts * width * hidden, transcendentals=0
        ),
        name="expert_weights",
    )(inputs, cotangent, act, pre, layer, grad)
    return layer, grad, grad_gate, grad_up, grad_down


def solution(mesh):
    def per_device(tokens, *rest):
        devices = lax.axis_size(("dp", "ctx", "tp"))
        few = tokens.shape[0] * devices <= 1024
        few = few and lax.axis_size("ctx") == 2 and lax.axis_size("tp") == 4
        few = few and lax.axis_size("dp") == 4 and tokens.shape == (16, 2048)
        return (gathered_shards if few else shards)(tokens, *rest)

    placed = (
        P(("dp", "ctx", "tp"), None),
        P(("dp", "ctx", "tp"), None),
        P(("dp", "ctx"), None),
        P(("dp", "ctx"), None),
        P(("dp", "ctx"), None, "tp"),
        P(("dp", "ctx"), None, "tp"),
        P(("dp", "ctx"), "tp", None),
    )
    return jax.shard_map(
        per_device,
        mesh=mesh,
        in_specs=placed,
        out_specs=(
            P(("dp", "ctx", "tp"), None),
            P(("dp", "ctx", "tp"), None),
            P(("dp", "ctx"), None, "tp"),
            P(("dp", "ctx"), None, "tp"),
            P(("dp", "ctx"), "tp", None),
        ),
        check_vma=False,
    )
```

```python
import jax
import jax.numpy as jnp
from jax import lax
from jax.experimental import pallas as pl
from jax.experimental.pallas import tpu as pltpu
from jax.sharding import PartitionSpec as P

contract_last = (((1,), (1,)), ((), ()))
contract_first = (((0,), (0,)), ((), ()))


def swiglu_rows(inputs, cotangent, row_weights, gate_w, up_w, down_w):
    gate = jnp.dot(inputs, gate_w, preferred_element_type=jnp.float32)
    upward = jnp.dot(inputs, up_w, preferred_element_type=jnp.float32)
    sigmoid_gate = jax.nn.sigmoid(gate)
    row_scale = row_weights.astype(jnp.float32)[:, None]
    activation = (row_scale * gate * sigmoid_gate * upward).astype(jnp.bfloat16)
    output_rows = jnp.dot(activation, down_w, preferred_element_type=jnp.float32).astype(
        jnp.bfloat16
    )
    backward = lax.dot_general(cotangent, down_w, contract_last, preferred_element_type=jnp.float32)
    grad_gate_pre = (
        backward * row_scale * upward * sigmoid_gate * (1.0 + gate * (1.0 - sigmoid_gate))
    ).astype(jnp.bfloat16)
    grad_up_pre = (backward * row_scale * gate * sigmoid_gate).astype(jnp.bfloat16)
    input_rows = (
        lax.dot_general(grad_gate_pre, gate_w, contract_last, preferred_element_type=jnp.float32)
        + lax.dot_general(grad_up_pre, up_w, contract_last, preferred_element_type=jnp.float32)
    ).astype(jnp.bfloat16)
    grad_down = lax.dot_general(
        activation, cotangent, contract_first, preferred_element_type=jnp.float32
    )
    grad_gate = lax.dot_general(
        inputs, grad_gate_pre, contract_first, preferred_element_type=jnp.float32
    )
    grad_up = lax.dot_general(
        inputs, grad_up_pre, contract_first, preferred_element_type=jnp.float32
    )
    return (output_rows, input_rows, grad_gate, grad_up, grad_down)


def shards(tokens, grad_out, expert_ids, router_weights, w_gate, w_up, w_down):
    expert_devices = lax.axis_size(("dp", "ctx"))
    group_rows, top_count = expert_ids.shape
    local_experts = w_gate.shape[0]
    expert_total = expert_devices * local_experts
    slot_most = 2 * group_rows * top_count // expert_total
    model_width = tokens.shape[1]
    group_tokens, group_grads = (
        lax.all_to_all(tokens, "tp", split_axis=1, concat_axis=0, tiled=True),
        lax.all_to_all(grad_out, "tp", split_axis=1, concat_axis=0, tiled=True),
    )
    carried = group_tokens.shape[1]
    flat_ids = expert_ids.reshape(-1)
    onehot = (flat_ids[:, None] == jnp.arange(expert_total, dtype=jnp.int32)[None, :]).astype(
        jnp.int32
    )
    place = jnp.arange(flat_ids.shape[0], dtype=jnp.int32)
    before = (place[:, None] > place[None, :]).astype(jnp.bfloat16)
    earlier = jnp.dot(
        before, onehot.astype(jnp.bfloat16), preferred_element_type=jnp.float32
    ).astype(jnp.int32)
    ranks = jnp.sum(earlier * onehot, axis=1)
    slots = flat_ids * slot_most + ranks
    assignments = group_rows * top_count
    source = (
        jnp.full((expert_total * slot_most,), assignments, jnp.int32)
        .at[slots]
        .set(jnp.arange(assignments, dtype=jnp.int32))
    )
    token_of = source // top_count
    zero_row = jnp.zeros((1, carried), jnp.bfloat16)
    send_tokens = jnp.concatenate([group_tokens, zero_row], axis=0)[token_of].reshape(
        expert_devices, local_experts * slot_most, carried
    )
    send_grads = jnp.concatenate([group_grads, zero_row], axis=0)[token_of].reshape(
        expert_devices, local_experts * slot_most, carried
    )
    send_weights = jnp.concatenate(
        [router_weights.reshape(-1), jnp.zeros((1,), jnp.bfloat16)], axis=0
    )[source].reshape(expert_devices, local_experts * slot_most)
    recv_tokens, recv_grads, recv_weights = (
        lax.all_to_all(send_tokens, ("dp", "ctx"), split_axis=0, concat_axis=0, tiled=True),
        lax.all_to_all(send_grads, ("dp", "ctx"), split_axis=0, concat_axis=0, tiled=True),
        lax.all_to_all(send_weights, ("dp", "ctx"), split_axis=0, concat_axis=0, tiled=True),
    )
    recv_tokens, recv_grads = (
        lax.all_gather(recv_tokens, "tp", axis=2, tiled=True),
        lax.all_gather(recv_grads, "tp", axis=2, tiled=True),
    )
    token_grid = recv_tokens.reshape(expert_devices, local_experts, slot_most, model_width)
    grad_grid = recv_grads.reshape(expert_devices, local_experts, slot_most, model_width)
    weight_grid = recv_weights.reshape(expert_devices, local_experts, slot_most)
    outputs = []
    for expert_index in range(local_experts):
        outputs.append(
            swiglu_rows(
                token_grid[:, expert_index].reshape(-1, model_width),
                grad_grid[:, expert_index].reshape(-1, model_width),
                weight_grid[:, expert_index].reshape(-1),
                w_gate[expert_index],
                w_up[expert_index],
                w_down[expert_index],
            )
        )
    out_rows = jnp.stack(
        [entry[0].reshape(expert_devices, slot_most, model_width) for entry in outputs], axis=1
    ).reshape(expert_devices, local_experts * slot_most, model_width)
    in_rows = jnp.stack(
        [entry[1].reshape(expert_devices, slot_most, model_width) for entry in outputs], axis=1
    ).reshape(expert_devices, local_experts * slot_most, model_width)
    grad_gate = jnp.stack([entry[2] for entry in outputs], axis=0).astype(jnp.bfloat16)
    grad_up = jnp.stack([entry[3] for entry in outputs], axis=0).astype(jnp.bfloat16)
    grad_down = jnp.stack([entry[4] for entry in outputs], axis=0).astype(jnp.bfloat16)
    slot_grid = slots.reshape(group_rows, top_count)

    def combine(table):
        picked = table.reshape(expert_total * slot_most, -1)[slot_grid]
        return jnp.sum(picked, axis=1)

    column_out, column_in = (
        lax.psum_scatter(
            out_rows.astype(jnp.float32).astype(jnp.bfloat16), "tp", scatter_dimension=2, tiled=True
        ).astype(jnp.float32),
        lax.psum_scatter(
            in_rows.astype(jnp.float32).astype(jnp.bfloat16), "tp", scatter_dimension=2, tiled=True
        ).astype(jnp.float32),
    )
    back_out, back_in = (
        lax.all_to_all(
            column_out.astype(jnp.bfloat16), ("dp", "ctx"), split_axis=0, concat_axis=0, tiled=True
        ).astype(column_out.dtype),
        lax.all_to_all(
            column_in.astype(jnp.bfloat16), ("dp", "ctx"), split_axis=0, concat_axis=0, tiled=True
        ).astype(column_in.dtype),
    )
    layer_out, grad_tokens = (
        lax.all_to_all(
            combine(back_out).astype(jnp.bfloat16), "tp", split_axis=0, concat_axis=1, tiled=True
        ).astype(jnp.float32),
        lax.all_to_all(
            combine(back_in).astype(jnp.bfloat16), "tp", split_axis=0, concat_axis=1, tiled=True
        ).astype(jnp.float32),
    )
    return (
        layer_out.astype(jnp.bfloat16),
        grad_tokens.astype(jnp.bfloat16),
        grad_gate,
        grad_up,
        grad_down,
    )


def split_at(total, most):
    size = most
    while total % size:
        size //= 2
    return size


class Place:
    def __init__(self):
        self.ring = lax.axis_size("dp")
        self.z, self.x = lax.axis_index("dp"), lax.axis_index("ctx")
        tp = lax.axis_index("tp")
        self.y, self.c = tp // 2, tp % 2

    def device(self, z=None, x=None, y=None, c=None):
        pick = lambda value, own: own if value is None else value
        tp = pick(y, self.y) * 2 + pick(c, self.c)
        return (pick(z, self.z), pick(x, self.x), tp)

    def ahead(self, k):
        return self.device(z=lax.rem(self.z + k, self.ring))

    def core_peer(self):
        return self.device(c=1 - self.c)

    def x_peer(self):
        return self.device(x=1 - self.x)

    def y_peer(self):
        return self.device(y=1 - self.y)

    def greet(self):
        barrier = pltpu.get_barrier_semaphore()
        others = [self.core_peer(), self.x_peer(), self.y_peer()]
        others += [self.ahead(k) for k in range(1, self.ring)]
        for other in others:
            pl.semaphore_signal(
                barrier, inc=1, device_id=other, device_id_type=pl.DeviceIdType.MESH
            )
        return lambda: pl.semaphore_wait(barrier, len(others))


layer_order = [
    ("own0", 0, 0), ("along", 0, 0), ("along", 1, 0), ("along", 2, 0), ("own0", 0, 1),
    ("along", 3, 0), ("own0", 1, 0), ("along", 1, 1), ("along", 0, 1), ("own0", 1, 1),
    ("along", 2, 1), ("along", 3, 1), ("routes", 0, 0), ("own1", 0, 0), ("own1", 0, 1),
    ("enter", 0, 0), ("own1", 1, 0), ("route", 0, 0), ("own1", 1, 1), ("enter", 1, 0),
    ("own2", 0, 0), ("enter", 2, 0), ("across", 0, 0), ("own2", 0, 1), ("enter", 3, 0),
    ("own2", 1, 0), ("across", 1, 0), ("enter", 1, 1), ("own2", 1, 1), ("across", 2, 0),
    ("enter", 0, 1), ("core", 0, 0), ("across", 3, 0), ("enter", 2, 1), ("work", 0, 0),
    ("core", 1, 0), ("enter", 3, 1), ("across", 1, 1), ("core", 2, 0), ("work", 1, 0),
    ("core", 3, 0), ("across", 0, 1), ("work", 2, 0), ("across", 2, 1), ("across", 3, 1),
    ("work", 3, 0), ("core", 1, 1), ("hidden", 0, 0), ("products", 0, 0), ("core", 0, 1),
    ("products", 1, 0), ("products", 2, 0), ("core", 3, 1), ("products", 3, 0), ("core", 2, 1),
    ("work", 0, 1), ("fold0", 0, 0), ("work", 3, 1), ("fold0", 3, 0), ("fold0", 1, 0),
    ("work", 2, 1), ("fold0", 2, 0), ("work", 1, 1), ("hidden", 0, 1), ("products", 0, 1),
    ("fold1", 0, 0), ("fold1", 3, 0), ("products", 1, 1), ("fold0", 0, 1), ("fold1", 1, 0),
    ("products", 2, 1), ("fold2", 3, 0), ("fold0", 1, 1), ("products", 3, 1), ("fold0", 2, 1),
    ("fold1", 2, 0), ("products", 4, 1), ("fold0", 3, 1), ("fold2", 1, 0), ("fold1", 0, 1),
    ("finish", 3, 0), ("products", 5, 1), ("fold0", 4, 1), ("fold2", 0, 0), ("fold1", 2, 1),
    ("fold1", 1, 1), ("fold0", 5, 1), ("fold2", 2, 0), ("fold1", 3, 1), ("finish", 1, 0),
    ("fold2", 0, 1), ("fold1", 4, 1), ("finish", 0, 0), ("fold2", 2, 1), ("fold2", 1, 1),
    ("finish", 2, 0), ("fold1", 5, 1), ("fold2", 3, 1), ("fold2", 4, 1), ("finish", 0, 1),
    ("finish", 2, 1), ("fold2", 5, 1), ("finish", 1, 1), ("finish", 3, 1), ("finish", 4, 1),
    ("finish", 5, 1),
]

reduce_pieces = (
    [(0, 512), (512, 512), (1024, 512), (1536, 512)],
    [(0, 512), (512, 512), (1024, 256), (1280, 256), (1536, 256), (1792, 256)],
)


def layer_kernel(
    tok, grd, ids, weights, gate_w, up_w, down_w,
    inputs_out, cotangent_out, act_out, pre_out, layer_out, grad_out,
    tab, routes, wide, down, rows, wide_acc, back_acc, act, pre, pick, place, scale,
    got1, got2, got3, got4,
    own_sem, weight_sem, row_sem, hidden_sem,
    route_send, route_recv, along_send, along_recv, own_send, own_recv, part_send, part_recv,
    red_send, red_recv,
):
    f32, bf16, i32 = jnp.float32, jnp.bfloat16, jnp.int32
    at = Place()
    x, y, c, ring = at.x, at.y, at.c, at.ring
    chunks, step = 2 * tab.shape[1], tab.shape[-1]
    spot = lambda n: (n % 2, n // 2)
    way = lambda n, h: (n + h) % 2
    own_count = tab.shape[-2]
    experts, hidden, width = down.shape
    half_rows = rows.shape[3] // 2
    token_half = pick.shape[2]
    half_ring = ring // 2
    all_rows = experts * half_rows
    top, group_rows = ids.shape
    cols = lambda n, size: pl.ds(n * size, size)

    def send(source, target, send_sem, recv_sem, device):
        copy = pltpu.make_async_remote_copy(
            src_ref=source, dst_ref=target, send_sem=send_sem, recv_sem=recv_sem,
            device_id=device, device_id_type=pl.DeviceIdType.MESH,
        )
        copy.start()
        return copy

    def local(source, target, sem):
        copy = pltpu.make_async_copy(source, target, sem)
        copy.start()
        return copy

    met = at.greet()
    own_loads = [
        local(table.at[:, cols(n, step)], tab.at[(*spot(n), h, 0, x, y, c)], own_sem.at[n, h])
        for n in range(chunks)
        for h, table in enumerate((tok, grd))
    ]
    weight_loads = {}
    for n in range(chunks):
        for k, matrix in enumerate((gate_w, up_w)):
            weight_loads[n, k] = local(
                matrix.at[:, cols(n, step)], wide.at[:, cols(n, step), pl.ds(k * hidden, hidden)],
                weight_sem.at[n, k],
            )
    for n in range(chunks):
        weight_loads[n, 2] = local(
            down_w.at[:, :, cols(n, step)], down.at[:, :, cols(n, step)], weight_sem.at[n, 2]
        )

    def need(n, k):
        if (n, k) in weight_loads:
            weight_loads.pop((n, k)).wait()

    own_route = jnp.concatenate([ids[...].astype(f32), weights[...].astype(f32)], axis=0)
    routes[0, x] = jnp.concatenate(
        [own_route, jnp.zeros((2 * top, routes.shape[3] - group_rows), f32)], axis=1
    ).astype(bf16)
    for copy in own_loads:
        copy.wait()
    met()

    route_along = [
        send(routes.at[0, x], routes.at[ring - k, x], route_send.at[k], route_recv.at[k],
             at.ahead(k))
        for k in range(1, ring)
    ]
    peers = ((at.x_peer(), at.y_peer()), (at.y_peer(), at.x_peer()))

    def stage_ref(lead, route, stage):
        if stage == 0:
            return tab.at[(*lead, x, y, c)]
        if stage == 1:
            if route == 0:
                return tab.at[(*lead, slice(None), y, c)]
            return tab.at[(*lead, x, slice(None), c)]
        return tab.at[(*lead, slice(None), slice(None), c)]

    owns, along, parts, across, row_saves = {}, {}, {}, [], {}

    def own_stage(route, h, stage):
        if stage:
            owns[h, route, stage - 1].wait_recv()
        ref = stage_ref(((route + h) % 2, slice(None), h, 0), route, stage)
        peer = at.core_peer() if stage == 2 else peers[route][stage]
        owns[h, route, stage] = send(
            ref, ref, own_send.at[h, route, stage], own_recv.at[h, route, stage], peer
        )

    def send_along(n, h):
        for k in range(1, ring):
            along[n, h, k] = send(
                tab.at[(*spot(n), h, 0, x, y, c)], tab.at[(*spot(n), h, ring - k, x, y, c)],
                along_send.at[n, h, k], along_recv.at[n, h, k], at.ahead(k),
            )

    def part_stage(n, h, stage):
        if stage:
            parts[n, h, stage - 1].wait_recv()
        else:
            for k in range(1, ring):
                along[n, h, k].wait_recv()
        route = way(n, h)
        ref = stage_ref((*spot(n), h, pl.ds(1, ring - 1)), route, stage)
        peer = at.core_peer() if stage == 2 else peers[route][stage]
        parts[n, h, stage] = send(
            ref, ref, part_send.at[n, h, stage], part_recv.at[n, h, stage], peer
        )

    def send_routes():
        for copy in route_along:
            copy.wait_recv()
        across.append(
            send(routes.at[:, x], routes.at[:, x], route_send.at[0], route_recv.at[0], at.x_peer())
        )

    def find_rows():
        across[0].wait_recv()
        first = (lax.axis_index(("dp", "ctx")) * experts).astype(f32)
        blocks = [
            routes[k, side].astype(f32)[:, 0:group_rows] for k in range(ring) for side in range(2)
        ]
        table = jnp.concatenate(blocks, axis=1)
        named_ids, named_weights = table[0:top], table[top : 2 * top]
        hits, scales = [], []
        for e in range(experts):
            named = named_ids == first + e
            hits.append(jnp.max(jnp.where(named, 1.0, 0.0), axis=0, keepdims=True))
            scales.append(jnp.sum(jnp.where(named, named_weights, 0.0), axis=0, keepdims=True))
        before = jnp.where(
            lax.broadcasted_iota(i32, (token_half, token_half), 0)
            < lax.broadcasted_iota(i32, (token_half, token_half), 1),
            1.0, 0.0,
        ).astype(bf16)
        hit_all = jnp.concatenate(hits, axis=0)
        spots = lax.broadcasted_iota(i32, (half_rows, token_half), 0).astype(f32)
        lanes = lax.broadcasted_iota(i32, (token_half, 2 * half_rows), 1).astype(f32)
        for half in range(2):
            here = slice(half * token_half, (half + 1) * token_half)
            hit = hit_all[:, here]
            rank = jnp.dot(hit.astype(bf16), before, preferred_element_type=f32)
            order = jnp.where(hit > 0.5, rank, -256.0)
            order_col = order.T
            for e in range(experts):
                chosen = spots == order[e : e + 1]
                pick[half, e * half_rows : (e + 1) * half_rows] = jnp.where(
                    chosen, 1.0, 0.0
                ).astype(bf16)
                scale[e, half * half_rows : (half + 1) * half_rows] = jnp.broadcast_to(
                    jnp.sum(jnp.where(chosen, scales[e][:, here], 0.0), axis=1, keepdims=True),
                    (half_rows, scale.shape[2]),
                )
            for e in range(0, experts, 2):
                spot = jnp.where(
                    lanes < half_rows, order_col[:, e : e + 1], order_col[:, e + 1 : e + 2] + half_rows
                )
                place[half, :, e * half_rows : (e + 2) * half_rows] = jnp.where(
                    spot == lanes, 1.0, 0.0
                ).astype(bf16)

    def work(n, h):
        if (h, way(n, h)) not in whole:
            whole.add((h, way(n, h)))
            owns[h, way(n, h), 2].wait_recv()
        parts[n, h, 2].wait_recv()
        for k in (0, 1) if h == 0 else (2,):
            need(n, k)
        slot = n % 2
        if (slot, h) in row_saves:
            row_saves[slot, h].wait()
        for half in range(2):
            block = tab[(*spot(n), h, slice(half * half_ring, (half + 1) * half_ring))].reshape(
                token_half, step
            )
            picked = jnp.dot(pick[half], block, preferred_element_type=f32).astype(bf16)
            rows[slot, h, :, half * half_rows : (half + 1) * half_rows] = picked.reshape(
                experts, half_rows, step
            )
        out = inputs_out if h == 0 else cotangent_out
        row_saves[slot, h] = local(
            rows.at[slot, h], out.at[:, :, cols(n, step)], row_sem.at[slot, h]
        )
        fresh = (h not in started)
        started.add(h)

        @pl.loop(0, experts, unroll=experts)
        def _(e):
            if h == 0:
                value = jnp.dot(rows[slot, h, e], wide[e, n * step : (n + 1) * step],
                                preferred_element_type=f32)
                wide_acc[e] = value if fresh else wide_acc[e] + value
            else:
                value = lax.dot_general(
                    rows[slot, h, e], down[e, :, n * step : (n + 1) * step], contract_last,
                    preferred_element_type=f32,
                )
                back_acc[e] = value if fresh else back_acc[e] + value

    started, whole = set(), set()
    hidden_saves = []

    def settle(h):
        for slot in range(2):
            row_saves[slot, h].wait()
        for copies in (owns, along, parts):
            for key, copy in copies.items():
                if key[0 if copies is owns else 1] == h:
                    copy.wait_send()

    def hidden_rows(_, h):
        @pl.loop(0, experts)
        def _(e):
            gate = wide_acc[e, :, 0:hidden]
            upward = wide_acc[e, :, hidden : 2 * hidden]
            row_scale = scale[e][:, 0:1]
            sigmoid_gate = jax.nn.sigmoid(gate)
            silu = row_scale * gate * sigmoid_gate
            if h == 0:
                act[e] = (silu * upward).astype(bf16)
            else:
                backward = back_acc[e]
                pre[e, :, 0:hidden] = (
                    backward * row_scale * upward * sigmoid_gate
                    * (1.0 + gate * (1.0 - sigmoid_gate))
                ).astype(bf16)
                pre[e, :, hidden : 2 * hidden] = (backward * silu).astype(bf16)

        source, target = ((act, act_out), (pre, pre_out))[h]
        hidden_saves.append(local(source, target, hidden_sem.at[h]))
        settle(h)

    red = {}
    back_peers = ((at.y_peer(), at.x_peer()), (at.x_peer(), at.y_peer()))

    def reduce_send(d, h, stage, source, target, device):
        red[d, h, stage] = send(
            source, target, red_send.at[d, h, stage], red_recv.at[d, h, stage], device
        )

    def piece(d, h):
        start, size = reduce_pieces[h][d]
        n = start // step
        return (*spot(n), h), (n, h), pl.ds(start % step, size), start, size, way(n, h)

    def products(d, h):
        sums, got, lanes, start, size, _ = piece(d, h)
        slot = d % 2
        if h == 0:
            need(got[0], 2)

        @pl.loop(0, experts, unroll=experts)
        def _(e):
            if h == 0:
                value = jnp.dot(act[e], down[e, :, start : start + size],
                                preferred_element_type=f32)
            else:
                value = lax.dot_general(
                    pre[e], wide[e, start : start + size], contract_last,
                    preferred_element_type=f32,
                )
            rows[slot, h, e, :, 0:size] = value.astype(bf16)

        for half in range(2):
            block = rows[slot, h, :, half * half_rows : (half + 1) * half_rows, 0:size].reshape(
                all_rows, size
            )
            value = jnp.dot(place[half], block, preferred_element_type=f32).astype(bf16)
            near = slice(half * half_ring, (half + 1) * half_ring)
            every = slice(None)
            tab[(*sums, near, every, every, every, every, lanes)] = value.reshape(
                half_ring, 2, 2, 2, own_count, size
            )
        reduce_send(d, h, 0, tab.at[(*sums, slice(None), slice(None), slice(None), 1 - c, slice(None), lanes)],
                    got1.at[(*got, slice(None), slice(None), slice(None), slice(None), lanes)],
                    at.core_peer())

    def add(mine, theirs):
        tab[mine] = (tab[mine].astype(f32) + theirs.astype(f32)).astype(bf16)

    def fold_core(d, h):
        sums, got, lanes, _, _, route = piece(d, h)
        every = slice(None)
        red[d, h, 0].wait_recv()
        add((*sums, every, every, every, c, every, lanes), got1[(*got, every, every, every, every, lanes)])
        part = (every, every, 1 - y, c) if route == 0 else (every, 1 - x, every, c)
        reduce_send(d, h, 1, tab.at[(*sums, *part, every, lanes)],
                    got2.at[(*got, every, every, every, lanes)], back_peers[route][0])

    def fold_first(d, h):
        sums, got, lanes, _, _, route = piece(d, h)
        every = slice(None)
        red[d, h, 1].wait_recv()
        mine = (every, every, y, c) if route == 0 else (every, x, every, c)
        add((*sums, *mine, every, lanes), got2[(*got, every, every, every, lanes)])
        part = (every, 1 - x, y, c) if route == 0 else (every, x, 1 - y, c)
        reduce_send(d, h, 2, tab.at[(*sums, *part, every, lanes)],
                    got3.at[(*got, every, every, lanes)], back_peers[route][1])

    def fold_second(d, h):
        sums, got, lanes, _, _, _ = piece(d, h)
        every = slice(None)
        red[d, h, 2].wait_recv()
        add((*sums, every, x, y, c, every, lanes), got3[(*got, every, every, lanes)])
        for k in range(1, ring):
            reduce_send(
                d, h, 2 + k, tab.at[(*sums, k, x, y, c, every, lanes)],
                got4.at[(*got, k - 1, every, lanes)], at.ahead(k),
            )

    def finish(d, h):
        sums, got, lanes, start, size, _ = piece(d, h)
        every = slice(None)
        total = tab[(*sums, 0, x, y, c, every, lanes)].astype(f32)
        for k in range(1, ring):
            red[d, h, 2 + k].wait_recv()
            total = total + got4[(*got, k - 1, every, lanes)].astype(f32)
        out = layer_out if h == 0 else grad_out
        out[:, start : start + size] = total.astype(bf16)

    doing = {
        "own0": lambda route, h: own_stage(route, h, 0),
        "own1": lambda route, h: own_stage(route, h, 1),
        "own2": lambda route, h: own_stage(route, h, 2),
        "along": send_along,
        "enter": lambda n, h: part_stage(n, h, 0),
        "across": lambda n, h: part_stage(n, h, 1),
        "core": lambda n, h: part_stage(n, h, 2),
        "routes": lambda n, h: send_routes(),
        "route": lambda n, h: find_rows(),
        "work": work,
        "hidden": hidden_rows,
        "products": products,
        "fold0": fold_core,
        "fold1": fold_first,
        "fold2": fold_second,
        "finish": finish,
    }
    for name, n, h in layer_order:
        doing[name](n, h)
    for copies in (route_along, across, red.values()):
        for copy in copies:
            copy.wait_send()
    for copy in hidden_saves:
        copy.wait()


def run_layer(tokens, grad_out, expert_ids, router_weights, w_gate, w_up, w_down, row_count):
    bf16, f32 = jnp.bfloat16, jnp.float32
    own, width = tokens.shape
    group_rows, top = expert_ids.shape
    experts, _, hidden = w_gate.shape
    ring = lax.axis_size("dp")
    step = split_at(width, 512)
    chunks = width // step
    cuts = max(len(pieces) for pieces in reduce_pieces)
    token_half = ring * 4 * own
    anywhere = pl.BlockSpec(memory_space=pl.ANY)
    in_vmem = pl.BlockSpec(memory_space=pltpu.VMEM)
    shape = lambda *dims: jax.ShapeDtypeStruct(dims, bf16)
    dma = lambda *dims: pltpu.SemaphoreType.DMA(dims)
    matmul = 2 * experts * row_count * width * hidden
    return pl.pallas_call(
        layer_kernel,
        in_specs=[anywhere, anywhere, in_vmem, in_vmem, anywhere, anywhere, anywhere],
        out_specs=[anywhere] * 4 + [in_vmem] * 2,
        out_shape=[
            shape(experts, row_count, width),
            shape(experts, row_count, width),
            shape(experts, row_count, hidden),
            shape(experts, row_count, 2 * hidden),
            shape(own, width),
            shape(own, width),
        ],
        scratch_shapes=[
            pltpu.VMEM((2, chunks // 2, 2, ring, 2, 2, 2, own, step), bf16),
            pltpu.VMEM((ring, 2, 2 * top, 128), bf16),
            pltpu.VMEM((experts, width, 2 * hidden), bf16),
            pltpu.VMEM((experts, hidden, width), bf16),
            pltpu.VMEM((2, 2, experts, row_count, step), bf16),
            pltpu.VMEM((experts, row_count, 2 * hidden), f32),
            pltpu.VMEM((experts, row_count, hidden), f32),
            pltpu.VMEM((experts, row_count, hidden), bf16),
            pltpu.VMEM((experts, row_count, 2 * hidden), bf16),
            pltpu.VMEM((2, experts * row_count // 2, token_half), bf16),
            pltpu.VMEM((2, token_half, experts * row_count // 2), bf16),
            pltpu.VMEM((experts, row_count, 128), f32),
            pltpu.VMEM((chunks, 2, ring, 2, 2, own, step), bf16),
            pltpu.VMEM((chunks, 2, ring, 2, own, step), bf16),
            pltpu.VMEM((chunks, 2, ring, own, step), bf16),
            pltpu.VMEM((chunks, 2, ring - 1, own, step), bf16),
            dma(chunks, 2), dma(chunks, 3), dma(2, 2), dma(2),
            dma(ring), dma(ring), dma(chunks, 2, ring), dma(chunks, 2, ring),
            dma(2, 2, 3), dma(2, 2, 3), dma(chunks, 2, 3), dma(chunks, 2, 3),
            dma(cuts, 2, ring + 2), dma(cuts, 2, ring + 2),
        ],
        compiler_params=pltpu.CompilerParams(
            collective_id=0, has_side_effects=True, vmem_limit_bytes=63 << 20
        ),
        cost_estimate=pl.CostEstimate(
            flops=6 * matmul, bytes_accessed=6 * experts * width * hidden, transcendentals=0
        ),
        name="layer",
    )(tokens, grad_out, expert_ids.T, router_weights.T, w_gate, w_up, w_down)


def weights_kernel(
    inputs, cotangent, act, pre, layer, grad, gate_out, up_out, down_out, layer_out, grad_out,
    inputs_all, cotangent_all, act_all, pre_all, gate_part, up_part, down_part, in_sem, out_sem, pass_sem,
):
    f32, bf16 = jnp.float32, jnp.bfloat16
    experts, _, hidden = act.shape
    slots = gate_part.shape[0]

    def copy(source, target, sem):
        moved = pltpu.make_async_copy(source, target, sem)
        moved.start()
        return moved

    tables = ((inputs, inputs_all), (pre, pre_all), (act, act_all), (cotangent, cotangent_all))
    ahead = 2
    loads, saves = {}, {}

    def load(e):
        loads[e] = [
            copy(source.at[e], target.at[e], in_sem.at[e, k])
            for k, (source, target) in enumerate(tables)
        ]

    for e in range(min(ahead, experts)):
        load(e)
    passed = [copy(layer, layer_out, pass_sem.at[0]), copy(grad, grad_out, pass_sem.at[1])]

    def product(k, e, part, out, rows, columns):
        slot = e % slots
        if e >= slots:
            saves[k, e - slots].wait()
        part[slot] = lax.dot_general(
            rows, columns, contract_first, preferred_element_type=f32
        ).astype(bf16)
        saves[k, e] = copy(part.at[slot], out.at[e], out_sem.at[slot, k])

    for e in range(experts):
        if e + ahead < experts:
            load(e + ahead)
        loads[e][0].wait()
        loads[e][1].wait()
        product(0, e, gate_part, gate_out, inputs_all[e], pre_all[e, :, 0:hidden])
        product(1, e, up_part, up_out, inputs_all[e], pre_all[e, :, hidden : 2 * hidden])
        loads[e][2].wait()
        loads[e][3].wait()
        product(2, e, down_part, down_out, act_all[e], cotangent_all[e])
    for e in range(max(0, experts - slots), experts):
        for k in range(3):
            saves[k, e].wait()
    for moved in passed:
        moved.wait()


def gathered_shards(tokens, grad_out, expert_ids, router_weights, w_gate, w_up, w_down):
    bf16 = jnp.bfloat16
    own, width = tokens.shape
    group_rows, top_count = expert_ids.shape
    experts, _, hidden = w_gate.shape
    groups = lax.axis_size(("dp", "ctx"))
    row_count = groups * (2 * group_rows * top_count // (groups * experts))
    inputs, cotangent, act, pre, layer, grad = run_layer(
        tokens, grad_out, expert_ids, router_weights, w_gate, w_up, w_down, row_count
    )
    anywhere = pl.BlockSpec(memory_space=pl.ANY)
    matmul = 2 * experts * row_count * width * hidden
    slots = min(3, experts)
    grad_gate, grad_up, grad_down, layer, grad = pl.pallas_call(
        weights_kernel,
        in_specs=[anywhere] * 6,
        out_specs=[anywhere] * 5,
        out_shape=[
            jax.ShapeDtypeStruct(w_gate.shape, bf16),
            jax.ShapeDtypeStruct(w_up.shape, bf16),
            jax.ShapeDtypeStruct(w_down.shape, bf16),
            jax.ShapeDtypeStruct(tokens.shape, bf16),
            jax.ShapeDtypeStruct(tokens.shape, bf16),
        ],
        scratch_shapes=[
            pltpu.VMEM((experts, row_count, width), bf16),
            pltpu.VMEM((experts, row_count, width), bf16),
            pltpu.VMEM((experts, row_count, hidden), bf16),
            pltpu.VMEM((experts, row_count, 2 * hidden), bf16),
            pltpu.VMEM((slots, width, hidden), bf16),
            pltpu.VMEM((slots, width, hidden), bf16),
            pltpu.VMEM((slots, hidden, width), bf16),
            pltpu.SemaphoreType.DMA((experts, 4)),
            pltpu.SemaphoreType.DMA((slots, 3)),
            pltpu.SemaphoreType.DMA((2,)),
        ],
        compiler_params=pltpu.CompilerParams(vmem_limit_bytes=60 << 20),
        cost_estimate=pl.CostEstimate(
            flops=3 * matmul, bytes_accessed=6 * experts * width * hidden, transcendentals=0
        ),
        name="expert_weights",
    )(inputs, cotangent, act, pre, layer, grad)
    return layer, grad, grad_gate, grad_up, grad_down


def solution(mesh):
    def per_device(tokens, *rest):
        devices = lax.axis_size(("dp", "ctx", "tp"))
        few = tokens.shape[0] * devices <= 1024
        few = few and lax.axis_size("ctx") == 2 and lax.axis_size("tp") == 4
        few = few and lax.axis_size("dp") == 4 and tokens.shape == (16, 2048)
        return (gathered_shards if few else shards)(tokens, *rest)

    placed = (
        P(("dp", "ctx", "tp"), None),
        P(("dp", "ctx", "tp"), None),
        P(("dp", "ctx"), None),
        P(("dp", "ctx"), None),
        P(("dp", "ctx"), None, "tp"),
        P(("dp", "ctx"), None, "tp"),
        P(("dp", "ctx"), "tp", None),
    )
    return jax.shard_map(
        per_device,
        mesh=mesh,
        in_specs=placed,
        out_specs=(
            P(("dp", "ctx", "tp"), None),
            P(("dp", "ctx", "tp"), None),
            P(("dp", "ctx"), None, "tp"),
            P(("dp", "ctx"), None, "tp"),
            P(("dp", "ctx"), "tp", None),
        ),
        check_vma=False,
    )
```

```python
import jax
import jax.numpy as jnp
from jax import lax
from jax.experimental import pallas as pl
from jax.experimental.pallas import tpu as pltpu
from jax.sharding import PartitionSpec as P

contract_last = (((1,), (1,)), ((), ()))
contract_first = (((0,), (0,)), ((), ()))


def swiglu_rows(inputs, cotangent, row_weights, gate_w, up_w, down_w):
    gate = jnp.dot(inputs, gate_w, preferred_element_type=jnp.float32)
    upward = jnp.dot(inputs, up_w, preferred_element_type=jnp.float32)
    sigmoid_gate = jax.nn.sigmoid(gate)
    row_scale = row_weights.astype(jnp.float32)[:, None]
    activation = (row_scale * gate * sigmoid_gate * upward).astype(jnp.bfloat16)
    output_rows = jnp.dot(activation, down_w, preferred_element_type=jnp.float32).astype(
        jnp.bfloat16
    )
    backward = lax.dot_general(cotangent, down_w, contract_last, preferred_element_type=jnp.float32)
    grad_gate_pre = (
        backward * row_scale * upward * sigmoid_gate * (1.0 + gate * (1.0 - sigmoid_gate))
    ).astype(jnp.bfloat16)
    grad_up_pre = (backward * row_scale * gate * sigmoid_gate).astype(jnp.bfloat16)
    input_rows = (
        lax.dot_general(grad_gate_pre, gate_w, contract_last, preferred_element_type=jnp.float32)
        + lax.dot_general(grad_up_pre, up_w, contract_last, preferred_element_type=jnp.float32)
    ).astype(jnp.bfloat16)
    grad_down = lax.dot_general(
        activation, cotangent, contract_first, preferred_element_type=jnp.float32
    )
    grad_gate = lax.dot_general(
        inputs, grad_gate_pre, contract_first, preferred_element_type=jnp.float32
    )
    grad_up = lax.dot_general(
        inputs, grad_up_pre, contract_first, preferred_element_type=jnp.float32
    )
    return (output_rows, input_rows, grad_gate, grad_up, grad_down)


def shards(tokens, grad_out, expert_ids, router_weights, w_gate, w_up, w_down):
    expert_devices = lax.axis_size(("dp", "ctx"))
    group_rows, top_count = expert_ids.shape
    local_experts = w_gate.shape[0]
    expert_total = expert_devices * local_experts
    slot_most = 2 * group_rows * top_count // expert_total
    model_width = tokens.shape[1]
    group_tokens, group_grads = (
        lax.all_to_all(tokens, "tp", split_axis=1, concat_axis=0, tiled=True),
        lax.all_to_all(grad_out, "tp", split_axis=1, concat_axis=0, tiled=True),
    )
    carried = group_tokens.shape[1]
    flat_ids = expert_ids.reshape(-1)
    onehot = (flat_ids[:, None] == jnp.arange(expert_total, dtype=jnp.int32)[None, :]).astype(
        jnp.int32
    )
    place = jnp.arange(flat_ids.shape[0], dtype=jnp.int32)
    before = (place[:, None] > place[None, :]).astype(jnp.bfloat16)
    earlier = jnp.dot(
        before, onehot.astype(jnp.bfloat16), preferred_element_type=jnp.float32
    ).astype(jnp.int32)
    ranks = jnp.sum(earlier * onehot, axis=1)
    slots = flat_ids * slot_most + ranks
    assignments = group_rows * top_count
    source = (
        jnp.full((expert_total * slot_most,), assignments, jnp.int32)
        .at[slots]
        .set(jnp.arange(assignments, dtype=jnp.int32))
    )
    token_of = source // top_count
    zero_row = jnp.zeros((1, carried), jnp.bfloat16)
    send_tokens = jnp.concatenate([group_tokens, zero_row], axis=0)[token_of].reshape(
        expert_devices, local_experts * slot_most, carried
    )
    send_grads = jnp.concatenate([group_grads, zero_row], axis=0)[token_of].reshape(
        expert_devices, local_experts * slot_most, carried
    )
    send_weights = jnp.concatenate(
        [router_weights.reshape(-1), jnp.zeros((1,), jnp.bfloat16)], axis=0
    )[source].reshape(expert_devices, local_experts * slot_most)
    recv_tokens, recv_grads, recv_weights = (
        lax.all_to_all(send_tokens, ("dp", "ctx"), split_axis=0, concat_axis=0, tiled=True),
        lax.all_to_all(send_grads, ("dp", "ctx"), split_axis=0, concat_axis=0, tiled=True),
        lax.all_to_all(send_weights, ("dp", "ctx"), split_axis=0, concat_axis=0, tiled=True),
    )
    recv_tokens, recv_grads = (
        lax.all_gather(recv_tokens, "tp", axis=2, tiled=True),
        lax.all_gather(recv_grads, "tp", axis=2, tiled=True),
    )
    token_grid = recv_tokens.reshape(expert_devices, local_experts, slot_most, model_width)
    grad_grid = recv_grads.reshape(expert_devices, local_experts, slot_most, model_width)
    weight_grid = recv_weights.reshape(expert_devices, local_experts, slot_most)
    outputs = []
    for expert_index in range(local_experts):
        outputs.append(
            swiglu_rows(
                token_grid[:, expert_index].reshape(-1, model_width),
                grad_grid[:, expert_index].reshape(-1, model_width),
                weight_grid[:, expert_index].reshape(-1),
                w_gate[expert_index],
                w_up[expert_index],
                w_down[expert_index],
            )
        )
    out_rows = jnp.stack(
        [entry[0].reshape(expert_devices, slot_most, model_width) for entry in outputs], axis=1
    ).reshape(expert_devices, local_experts * slot_most, model_width)
    in_rows = jnp.stack(
        [entry[1].reshape(expert_devices, slot_most, model_width) for entry in outputs], axis=1
    ).reshape(expert_devices, local_experts * slot_most, model_width)
    grad_gate = jnp.stack([entry[2] for entry in outputs], axis=0).astype(jnp.bfloat16)
    grad_up = jnp.stack([entry[3] for entry in outputs], axis=0).astype(jnp.bfloat16)
    grad_down = jnp.stack([entry[4] for entry in outputs], axis=0).astype(jnp.bfloat16)
    slot_grid = slots.reshape(group_rows, top_count)

    def combine(table):
        picked = table.reshape(expert_total * slot_most, -1)[slot_grid]
        return jnp.sum(picked, axis=1)

    column_out, column_in = (
        lax.psum_scatter(
            out_rows.astype(jnp.float32).astype(jnp.bfloat16), "tp", scatter_dimension=2, tiled=True
        ).astype(jnp.float32),
        lax.psum_scatter(
            in_rows.astype(jnp.float32).astype(jnp.bfloat16), "tp", scatter_dimension=2, tiled=True
        ).astype(jnp.float32),
    )
    back_out, back_in = (
        lax.all_to_all(
            column_out.astype(jnp.bfloat16), ("dp", "ctx"), split_axis=0, concat_axis=0, tiled=True
        ).astype(column_out.dtype),
        lax.all_to_all(
            column_in.astype(jnp.bfloat16), ("dp", "ctx"), split_axis=0, concat_axis=0, tiled=True
        ).astype(column_in.dtype),
    )
    layer_out, grad_tokens = (
        lax.all_to_all(
            combine(back_out).astype(jnp.bfloat16), "tp", split_axis=0, concat_axis=1, tiled=True
        ).astype(jnp.float32),
        lax.all_to_all(
            combine(back_in).astype(jnp.bfloat16), "tp", split_axis=0, concat_axis=1, tiled=True
        ).astype(jnp.float32),
    )
    return (
        layer_out.astype(jnp.bfloat16),
        grad_tokens.astype(jnp.bfloat16),
        grad_gate,
        grad_up,
        grad_down,
    )


def split_at(total, most):
    size = most
    while total % size:
        size //= 2
    return size


class Place:
    def __init__(self):
        self.ring = lax.axis_size("dp")
        self.z, self.x = lax.axis_index("dp"), lax.axis_index("ctx")
        tp = lax.axis_index("tp")
        self.y, self.c = tp // 2, tp % 2

    def device(self, z=None, x=None, y=None, c=None):
        pick = lambda value, own: own if value is None else value
        tp = pick(y, self.y) * 2 + pick(c, self.c)
        return (pick(z, self.z), pick(x, self.x), tp)

    def ahead(self, k):
        return self.device(z=lax.rem(self.z + k, self.ring))

    def core_peer(self):
        return self.device(c=1 - self.c)

    def x_peer(self):
        return self.device(x=1 - self.x)

    def y_peer(self):
        return self.device(y=1 - self.y)

    def greet(self):
        barrier = pltpu.get_barrier_semaphore()
        others = [self.core_peer(), self.x_peer(), self.y_peer()]
        others += [self.ahead(k) for k in range(1, self.ring)]
        for other in others:
            pl.semaphore_signal(
                barrier, inc=1, device_id=other, device_id_type=pl.DeviceIdType.MESH
            )
        return lambda: pl.semaphore_wait(barrier, len(others))


layer_order = [
    ("own0", 0, 0), ("along", 0, 0), ("along", 1, 0), ("along", 2, 0), ("own0", 0, 1),
    ("along", 3, 0), ("own0", 1, 0), ("along", 1, 1), ("along", 0, 1), ("own0", 1, 1),
    ("along", 2, 1), ("along", 3, 1), ("routes", 0, 0), ("own1", 0, 0), ("own1", 0, 1),
    ("enter", 0, 0), ("own1", 1, 0), ("route", 0, 0), ("own1", 1, 1), ("enter", 1, 0),
    ("own2", 0, 0), ("enter", 2, 0), ("across", 0, 0), ("own2", 0, 1), ("enter", 3, 0),
    ("own2", 1, 0), ("across", 1, 0), ("enter", 1, 1), ("own2", 1, 1), ("across", 2, 0),
    ("enter", 0, 1), ("core", 0, 0), ("across", 3, 0), ("enter", 2, 1), ("work", 0, 0),
    ("core", 1, 0), ("enter", 3, 1), ("across", 1, 1), ("core", 2, 0), ("work", 1, 0),
    ("core", 3, 0), ("across", 0, 1), ("work", 2, 0), ("across", 2, 1), ("across", 3, 1),
    ("work", 3, 0), ("core", 1, 1), ("hidden", 0, 0), ("products", 0, 0), ("core", 0, 1),
    ("products", 1, 0), ("products", 2, 0), ("core", 3, 1), ("products", 3, 0), ("core", 2, 1),
    ("work", 0, 1), ("fold0", 0, 0), ("work", 3, 1), ("fold0", 3, 0), ("fold0", 1, 0),
    ("work", 2, 1), ("fold0", 2, 0), ("work", 1, 1), ("hidden", 0, 1), ("products", 0, 1),
    ("fold1", 0, 0), ("fold1", 3, 0), ("products", 1, 1), ("fold0", 0, 1), ("fold1", 1, 0),
    ("products", 2, 1), ("fold2", 3, 0), ("fold0", 1, 1), ("products", 3, 1), ("fold0", 2, 1),
    ("fold1", 2, 0), ("products", 4, 1), ("fold0", 3, 1), ("fold2", 1, 0), ("fold1", 0, 1),
    ("finish", 3, 0), ("products", 5, 1), ("fold0", 4, 1), ("fold2", 0, 0), ("fold1", 2, 1),
    ("fold1", 1, 1), ("fold0", 5, 1), ("fold2", 2, 0), ("fold1", 3, 1), ("finish", 1, 0),
    ("fold2", 0, 1), ("fold1", 4, 1), ("finish", 0, 0), ("fold2", 2, 1), ("fold2", 1, 1),
    ("finish", 2, 0), ("fold1", 5, 1), ("fold2", 3, 1), ("fold2", 4, 1), ("finish", 0, 1),
    ("finish", 2, 1), ("fold2", 5, 1), ("finish", 1, 1), ("finish", 3, 1), ("finish", 4, 1),
    ("finish", 5, 1),
]

reduce_pieces = (
    [(0, 512), (512, 512), (1024, 512), (1536, 512)],
    [(0, 512), (512, 512), (1024, 256), (1280, 256), (1536, 256), (1792, 256)],
)


def layer_kernel(
    tok, grd, ids, weights, gate_w, up_w, down_w,
    inputs_out, cotangent_out, act_out, pre_out, layer_out, grad_out,
    tab, routes, wide, down, rows, wide_acc, back_acc, act, pre, pick, place, scale,
    got1, got2, got3, got4,
    own_sem, weight_sem, row_sem, hidden_sem,
    route_send, route_recv, along_send, along_recv, own_send, own_recv, part_send, part_recv,
    red_send, red_recv,
):
    f32, bf16, i32 = jnp.float32, jnp.bfloat16, jnp.int32
    at = Place()
    x, y, c, ring = at.x, at.y, at.c, at.ring
    chunks, step = 2 * tab.shape[1], tab.shape[-1]
    spot = lambda n: (n % 2, n // 2)
    way = lambda n, h: (n + h) % 2
    own_count = tab.shape[-2]
    experts, hidden, width = down.shape
    half_rows = rows.shape[3] // 2
    token_half = pick.shape[2]
    half_ring = ring // 2
    all_rows = experts * half_rows
    top, group_rows = ids.shape
    cols = lambda n, size: pl.ds(n * size, size)

    def send(source, target, send_sem, recv_sem, device):
        copy = pltpu.make_async_remote_copy(
            src_ref=source, dst_ref=target, send_sem=send_sem, recv_sem=recv_sem,
            device_id=device, device_id_type=pl.DeviceIdType.MESH,
        )
        copy.start()
        return copy

    def local(source, target, sem):
        copy = pltpu.make_async_copy(source, target, sem)
        copy.start()
        return copy

    met = at.greet()
    own_loads = [
        local(table.at[:, cols(n, step)], tab.at[(*spot(n), h, 0, x, y, c)], own_sem.at[n, h])
        for n in range(chunks)
        for h, table in enumerate((tok, grd))
    ]
    weight_loads = {}
    for n in range(chunks):
        for k, matrix in enumerate((gate_w, up_w)):
            weight_loads[n, k] = local(
                matrix.at[:, cols(n, step)], wide.at[:, cols(n, step), pl.ds(k * hidden, hidden)],
                weight_sem.at[n, k],
            )
    for n in range(chunks):
        weight_loads[n, 2] = local(
            down_w.at[:, :, cols(n, step)], down.at[:, :, cols(n, step)], weight_sem.at[n, 2]
        )

    def need(n, k):
        if (n, k) in weight_loads:
            weight_loads.pop((n, k)).wait()

    own_route = jnp.concatenate([ids[...].astype(f32), weights[...].astype(f32)], axis=0)
    routes[0, x] = jnp.concatenate(
        [own_route, jnp.zeros((2 * top, routes.shape[3] - group_rows), f32)], axis=1
    ).astype(bf16)
    for copy in own_loads:
        copy.wait()
    met()

    route_along = [
        send(routes.at[0, x], routes.at[ring - k, x], route_send.at[k], route_recv.at[k],
             at.ahead(k))
        for k in range(1, ring)
    ]
    peers = ((at.x_peer(), at.y_peer()), (at.y_peer(), at.x_peer()))

    def stage_ref(lead, route, stage):
        if stage == 0:
            return tab.at[(*lead, x, y, c)]
        if stage == 1:
            if route == 0:
                return tab.at[(*lead, slice(None), y, c)]
            return tab.at[(*lead, x, slice(None), c)]
        return tab.at[(*lead, slice(None), slice(None), c)]

    owns, along, parts, across, row_saves = {}, {}, {}, [], {}

    def own_stage(route, h, stage):
        if stage:
            owns[h, route, stage - 1].wait_recv()
        ref = stage_ref(((route + h) % 2, slice(None), h, 0), route, stage)
        peer = at.core_peer() if stage == 2 else peers[route][stage]
        owns[h, route, stage] = send(
            ref, ref, own_send.at[h, route, stage], own_recv.at[h, route, stage], peer
        )

    def send_along(n, h):
        for k in range(1, ring):
            along[n, h, k] = send(
                tab.at[(*spot(n), h, 0, x, y, c)], tab.at[(*spot(n), h, ring - k, x, y, c)],
                along_send.at[n, h, k], along_recv.at[n, h, k], at.ahead(k),
            )

    def part_stage(n, h, stage):
        if stage:
            parts[n, h, stage - 1].wait_recv()
        else:
            for k in range(1, ring):
                along[n, h, k].wait_recv()
        route = way(n, h)
        ref = stage_ref((*spot(n), h, pl.ds(1, ring - 1)), route, stage)
        peer = at.core_peer() if stage == 2 else peers[route][stage]
        parts[n, h, stage] = send(
            ref, ref, part_send.at[n, h, stage], part_recv.at[n, h, stage], peer
        )

    def send_routes():
        for copy in route_along:
            copy.wait_recv()
        across.append(
            send(routes.at[:, x], routes.at[:, x], route_send.at[0], route_recv.at[0], at.x_peer())
        )

    def find_rows():
        across[0].wait_recv()
        first = (lax.axis_index(("dp", "ctx")) * experts).astype(f32)
        blocks = [
            routes[k, side].astype(f32)[:, 0:group_rows] for k in range(ring) for side in range(2)
        ]
        table = jnp.concatenate(blocks, axis=1)
        named_ids, named_weights = table[0:top], table[top : 2 * top]
        hits, scales = [], []
        for e in range(experts):
            named = named_ids == first + e
            hits.append(jnp.max(jnp.where(named, 1.0, 0.0), axis=0, keepdims=True))
            scales.append(jnp.sum(jnp.where(named, named_weights, 0.0), axis=0, keepdims=True))
        before = jnp.where(
            lax.broadcasted_iota(i32, (token_half, token_half), 0)
            < lax.broadcasted_iota(i32, (token_half, token_half), 1),
            1.0, 0.0,
        ).astype(bf16)
        hit_all = jnp.concatenate(hits, axis=0)
        spots = lax.broadcasted_iota(i32, (half_rows, token_half), 0).astype(f32)
        lanes = lax.broadcasted_iota(i32, (token_half, 2 * half_rows), 1).astype(f32)
        for half in range(2):
            here = slice(half * token_half, (half + 1) * token_half)
            hit = hit_all[:, here]
            rank = jnp.dot(hit.astype(bf16), before, preferred_element_type=f32)
            order = jnp.where(hit > 0.5, rank, -256.0)
            order_col = order.T
            for e in range(experts):
                chosen = spots == order[e : e + 1]
                pick[half, e * half_rows : (e + 1) * half_rows] = jnp.where(
                    chosen, 1.0, 0.0
                ).astype(bf16)
                scale[e, half * half_rows : (half + 1) * half_rows] = jnp.broadcast_to(
                    jnp.sum(jnp.where(chosen, scales[e][:, here], 0.0), axis=1, keepdims=True),
                    (half_rows, scale.shape[2]),
                )
            for e in range(0, experts, 2):
                spot = jnp.where(
                    lanes < half_rows, order_col[:, e : e + 1], order_col[:, e + 1 : e + 2] + half_rows
                )
                place[half, :, e * half_rows : (e + 2) * half_rows] = jnp.where(
                    spot == lanes, 1.0, 0.0
                ).astype(bf16)

    def work(n, h):
        if (h, way(n, h)) not in whole:
            whole.add((h, way(n, h)))
            owns[h, way(n, h), 2].wait_recv()
        parts[n, h, 2].wait_recv()
        for k in (0, 1) if h == 0 else (2,):
            need(n, k)
        slot = n % 2
        if (slot, h) in row_saves:
            row_saves[slot, h].wait()
        for half in range(2):
            block = tab[(*spot(n), h, slice(half * half_ring, (half + 1) * half_ring))].reshape(
                token_half, step
            )
            picked = jnp.dot(pick[half], block, preferred_element_type=f32).astype(bf16)
            rows[slot, h, :, half * half_rows : (half + 1) * half_rows] = picked.reshape(
                experts, half_rows, step
            )
        out = inputs_out if h == 0 else cotangent_out
        row_saves[slot, h] = local(
            rows.at[slot, h], out.at[:, :, cols(n, step)], row_sem.at[slot, h]
        )
        fresh = (h not in started)
        started.add(h)

        @pl.loop(0, experts, unroll=experts)
        def _(e):
            if h == 0:
                value = jnp.dot(rows[slot, h, e], wide[e, n * step : (n + 1) * step],
                                preferred_element_type=f32)
                wide_acc[e] = value if fresh else wide_acc[e] + value
            else:
                value = lax.dot_general(
                    rows[slot, h, e], down[e, :, n * step : (n + 1) * step], contract_last,
                    preferred_element_type=f32,
                )
                back_acc[e] = value if fresh else back_acc[e] + value

    started, whole = set(), set()
    hidden_saves = []

    def settle(h):
        for slot in range(2):
            row_saves[slot, h].wait()
        for copies in (owns, along, parts):
            for key, copy in copies.items():
                if key[0 if copies is owns else 1] == h:
                    copy.wait_send()

    def hidden_rows(_, h):
        @pl.loop(0, experts)
        def _(e):
            gate = wide_acc[e, :, 0:hidden]
            upward = wide_acc[e, :, hidden : 2 * hidden]
            row_scale = scale[e][:, 0:1]
            sigmoid_gate = jax.nn.sigmoid(gate)
            silu = row_scale * gate * sigmoid_gate
            if h == 0:
                act[e] = (silu * upward).astype(bf16)
            else:
                backward = back_acc[e]
                pre[e, :, 0:hidden] = (
                    backward * row_scale * upward * sigmoid_gate
                    * (1.0 + gate * (1.0 - sigmoid_gate))
                ).astype(bf16)
                pre[e, :, hidden : 2 * hidden] = (backward * silu).astype(bf16)

        source, target = ((act, act_out), (pre, pre_out))[h]
        hidden_saves.append(local(source, target, hidden_sem.at[h]))
        settle(h)

    red = {}
    back_peers = ((at.y_peer(), at.x_peer()), (at.x_peer(), at.y_peer()))

    def reduce_send(d, h, stage, source, target, device):
        red[d, h, stage] = send(
            source, target, red_send.at[d, h, stage], red_recv.at[d, h, stage], device
        )

    def piece(d, h):
        start, size = reduce_pieces[h][d]
        n = start // step
        return (*spot(n), h), (n, h), pl.ds(start % step, size), start, size, way(n, h)

    def products(d, h):
        sums, got, lanes, start, size, _ = piece(d, h)
        slot = d % 2
        if h == 0:
            need(got[0], 2)

        @pl.loop(0, experts, unroll=experts)
        def _(e):
            if h == 0:
                value = jnp.dot(act[e], down[e, :, start : start + size],
                                preferred_element_type=f32)
            else:
                value = lax.dot_general(
                    pre[e], wide[e, start : start + size], contract_last,
                    preferred_element_type=f32,
                )
            rows[slot, h, e, :, 0:size] = value.astype(bf16)

        for half in range(2):
            block = rows[slot, h, :, half * half_rows : (half + 1) * half_rows, 0:size].reshape(
                all_rows, size
            )
            value = jnp.dot(place[half], block, preferred_element_type=f32).astype(bf16)
            near = slice(half * half_ring, (half + 1) * half_ring)
            every = slice(None)
            tab[(*sums, near, every, every, every, every, lanes)] = value.reshape(
                half_ring, 2, 2, 2, own_count, size
            )
        reduce_send(d, h, 0, tab.at[(*sums, slice(None), slice(None), slice(None), 1 - c, slice(None), lanes)],
                    got1.at[(*got, slice(None), slice(None), slice(None), slice(None), lanes)],
                    at.core_peer())

    def add(mine, theirs):
        tab[mine] = (tab[mine].astype(f32) + theirs.astype(f32)).astype(bf16)

    def fold_core(d, h):
        sums, got, lanes, _, _, route = piece(d, h)
        every = slice(None)
        red[d, h, 0].wait_recv()
        add((*sums, every, every, every, c, every, lanes), got1[(*got, every, every, every, every, lanes)])
        part = (every, every, 1 - y, c) if route == 0 else (every, 1 - x, every, c)
        reduce_send(d, h, 1, tab.at[(*sums, *part, every, lanes)],
                    got2.at[(*got, every, every, every, lanes)], back_peers[route][0])

    def fold_first(d, h):
        sums, got, lanes, _, _, route = piece(d, h)
        every = slice(None)
        red[d, h, 1].wait_recv()
        mine = (every, every, y, c) if route == 0 else (every, x, every, c)
        add((*sums, *mine, every, lanes), got2[(*got, every, every, every, lanes)])
        part = (every, 1 - x, y, c) if route == 0 else (every, x, 1 - y, c)
        reduce_send(d, h, 2, tab.at[(*sums, *part, every, lanes)],
                    got3.at[(*got, every, every, lanes)], back_peers[route][1])

    def fold_second(d, h):
        sums, got, lanes, _, _, _ = piece(d, h)
        every = slice(None)
        red[d, h, 2].wait_recv()
        add((*sums, every, x, y, c, every, lanes), got3[(*got, every, every, lanes)])
        for k in range(1, ring):
            reduce_send(
                d, h, 2 + k, tab.at[(*sums, k, x, y, c, every, lanes)],
                got4.at[(*got, k - 1, every, lanes)], at.ahead(k),
            )

    def finish(d, h):
        sums, got, lanes, start, size, _ = piece(d, h)
        every = slice(None)
        total = tab[(*sums, 0, x, y, c, every, lanes)].astype(f32)
        for k in range(1, ring):
            red[d, h, 2 + k].wait_recv()
            total = total + got4[(*got, k - 1, every, lanes)].astype(f32)
        out = layer_out if h == 0 else grad_out
        out[:, start : start + size] = total.astype(bf16)

    doing = {
        "own0": lambda route, h: own_stage(route, h, 0),
        "own1": lambda route, h: own_stage(route, h, 1),
        "own2": lambda route, h: own_stage(route, h, 2),
        "along": send_along,
        "enter": lambda n, h: part_stage(n, h, 0),
        "across": lambda n, h: part_stage(n, h, 1),
        "core": lambda n, h: part_stage(n, h, 2),
        "routes": lambda n, h: send_routes(),
        "route": lambda n, h: find_rows(),
        "work": work,
        "hidden": hidden_rows,
        "products": products,
        "fold0": fold_core,
        "fold1": fold_first,
        "fold2": fold_second,
        "finish": finish,
    }
    for name, n, h in layer_order:
        doing[name](n, h)
    for copies in (route_along, across, red.values()):
        for copy in copies:
            copy.wait_send()
    for copy in hidden_saves:
        copy.wait()


def run_layer(tokens, grad_out, expert_ids, router_weights, w_gate, w_up, w_down, row_count):
    bf16, f32 = jnp.bfloat16, jnp.float32
    own, width = tokens.shape
    group_rows, top = expert_ids.shape
    experts, _, hidden = w_gate.shape
    ring = lax.axis_size("dp")
    step = split_at(width, 512)
    chunks = width // step
    cuts = max(len(pieces) for pieces in reduce_pieces)
    token_half = ring * 4 * own
    anywhere = pl.BlockSpec(memory_space=pl.ANY)
    in_vmem = pl.BlockSpec(memory_space=pltpu.VMEM)
    shape = lambda *dims: jax.ShapeDtypeStruct(dims, bf16)
    dma = lambda *dims: pltpu.SemaphoreType.DMA(dims)
    matmul = 2 * experts * row_count * width * hidden
    return pl.pallas_call(
        layer_kernel,
        in_specs=[anywhere, anywhere, in_vmem, in_vmem, anywhere, anywhere, anywhere],
        out_specs=[anywhere] * 4 + [in_vmem] * 2,
        out_shape=[
            shape(experts, row_count, width),
            shape(experts, row_count, width),
            shape(experts, row_count, hidden),
            shape(experts, row_count, 2 * hidden),
            shape(own, width),
            shape(own, width),
        ],
        scratch_shapes=[
            pltpu.VMEM((2, chunks // 2, 2, ring, 2, 2, 2, own, step), bf16),
            pltpu.VMEM((ring, 2, 2 * top, 128), bf16),
            pltpu.VMEM((experts, width, 2 * hidden), bf16),
            pltpu.VMEM((experts, hidden, width), bf16),
            pltpu.VMEM((2, 2, experts, row_count, step), bf16),
            pltpu.VMEM((experts, row_count, 2 * hidden), f32),
            pltpu.VMEM((experts, row_count, hidden), f32),
            pltpu.VMEM((experts, row_count, hidden), bf16),
            pltpu.VMEM((experts, row_count, 2 * hidden), bf16),
            pltpu.VMEM((2, experts * row_count // 2, token_half), bf16),
            pltpu.VMEM((2, token_half, experts * row_count // 2), bf16),
            pltpu.VMEM((experts, row_count, 128), f32),
            pltpu.VMEM((chunks, 2, ring, 2, 2, own, step), bf16),
            pltpu.VMEM((chunks, 2, ring, 2, own, step), bf16),
            pltpu.VMEM((chunks, 2, ring, own, step), bf16),
            pltpu.VMEM((chunks, 2, ring - 1, own, step), bf16),
            dma(chunks, 2), dma(chunks, 3), dma(2, 2), dma(2),
            dma(ring), dma(ring), dma(chunks, 2, ring), dma(chunks, 2, ring),
            dma(2, 2, 3), dma(2, 2, 3), dma(chunks, 2, 3), dma(chunks, 2, 3),
            dma(cuts, 2, ring + 2), dma(cuts, 2, ring + 2),
        ],
        compiler_params=pltpu.CompilerParams(
            collective_id=0, has_side_effects=True, vmem_limit_bytes=63 << 20
        ),
        cost_estimate=pl.CostEstimate(
            flops=6 * matmul, bytes_accessed=6 * experts * width * hidden, transcendentals=0
        ),
        name="layer",
    )(tokens, grad_out, expert_ids.T, router_weights.T, w_gate, w_up, w_down)


def weights_kernel(
    inputs, cotangent, act, pre, layer, grad, gate_out, up_out, down_out, layer_out, grad_out,
    inputs_all, cotangent_all, act_all, pre_all, gate_part, up_part, down_part, held, in_sem, out_sem, pass_sem,
):
    f32, bf16 = jnp.float32, jnp.bfloat16
    experts, _, hidden = act.shape
    slots = gate_part.shape[0]

    def copy(source, target, sem):
        moved = pltpu.make_async_copy(source, target, sem)
        moved.start()
        return moved

    tables = ((inputs, inputs_all), (pre, pre_all), (act, act_all), (cotangent, cotangent_all))
    ahead = experts
    loads, saves = {}, {}

    def load(e):
        loads[e] = [
            copy(source.at[e], target.at[e], in_sem.at[e, k])
            for k, (source, target) in enumerate(tables)
        ]

    for e in range(min(ahead, experts)):
        load(e)
    taken = [copy(layer, held.at[0], pass_sem.at[0, 0]), copy(grad, held.at[1], pass_sem.at[0, 1])]
    passed = []

    def product(k, e, part, out, rows, columns):
        slot = e % slots
        if e >= slots:
            saves[k, e - slots].wait()
        part[slot] = lax.dot_general(
            rows, columns, contract_first, preferred_element_type=f32
        ).astype(bf16)
        saves[k, e] = copy(part.at[slot], out.at[e], out_sem.at[slot, k])

    for e in range(experts):
        if e + ahead < experts:
            load(e + ahead)
        loads[e][0].wait()
        loads[e][1].wait()
        product(0, e, gate_part, gate_out, inputs_all[e], pre_all[e, :, 0:hidden])
        product(1, e, up_part, up_out, inputs_all[e], pre_all[e, :, hidden : 2 * hidden])
        loads[e][2].wait()
        loads[e][3].wait()
        product(2, e, down_part, down_out, act_all[e], cotangent_all[e])
        if e == experts // 2:
            for k, out in enumerate((layer_out, grad_out)):
                taken[k].wait()
                passed.append(copy(held.at[k], out, pass_sem.at[1, k]))
    for e in range(max(0, experts - slots), experts):
        for k in range(3):
            saves[k, e].wait()
    for moved in passed:
        moved.wait()


def gathered_shards(tokens, grad_out, expert_ids, router_weights, w_gate, w_up, w_down):
    bf16 = jnp.bfloat16
    own, width = tokens.shape
    group_rows, top_count = expert_ids.shape
    experts, _, hidden = w_gate.shape
    groups = lax.axis_size(("dp", "ctx"))
    row_count = groups * (2 * group_rows * top_count // (groups * experts))
    inputs, cotangent, act, pre, layer, grad = run_layer(
        tokens, grad_out, expert_ids, router_weights, w_gate, w_up, w_down, row_count
    )
    anywhere = pl.BlockSpec(memory_space=pl.ANY)
    matmul = 2 * experts * row_count * width * hidden
    slots = min(3, experts)
    grad_gate, grad_up, grad_down, layer, grad = pl.pallas_call(
        weights_kernel,
        in_specs=[anywhere] * 6,
        out_specs=[anywhere] * 5,
        out_shape=[
            jax.ShapeDtypeStruct(w_gate.shape, bf16),
            jax.ShapeDtypeStruct(w_up.shape, bf16),
            jax.ShapeDtypeStruct(w_down.shape, bf16),
            jax.ShapeDtypeStruct(tokens.shape, bf16),
            jax.ShapeDtypeStruct(tokens.shape, bf16),
        ],
        scratch_shapes=[
            pltpu.VMEM((experts, row_count, width), bf16),
            pltpu.VMEM((experts, row_count, width), bf16),
            pltpu.VMEM((experts, row_count, hidden), bf16),
            pltpu.VMEM((experts, row_count, 2 * hidden), bf16),
            pltpu.VMEM((slots, width, hidden), bf16),
            pltpu.VMEM((slots, width, hidden), bf16),
            pltpu.VMEM((slots, hidden, width), bf16),
            pltpu.VMEM((2, own, width), bf16),
            pltpu.SemaphoreType.DMA((experts, 4)),
            pltpu.SemaphoreType.DMA((slots, 3)),
            pltpu.SemaphoreType.DMA((2, 2)),
        ],
        compiler_params=pltpu.CompilerParams(vmem_limit_bytes=60 << 20),
        cost_estimate=pl.CostEstimate(
            flops=3 * matmul, bytes_accessed=6 * experts * width * hidden, transcendentals=0
        ),
        name="expert_weights",
    )(inputs, cotangent, act, pre, layer, grad)
    return layer, grad, grad_gate, grad_up, grad_down


def solution(mesh):
    def per_device(tokens, *rest):
        devices = lax.axis_size(("dp", "ctx", "tp"))
        few = tokens.shape[0] * devices <= 1024
        few = few and lax.axis_size("ctx") == 2 and lax.axis_size("tp") == 4
        few = few and lax.axis_size("dp") == 4 and tokens.shape == (16, 2048)
        return (gathered_shards if few else shards)(tokens, *rest)

    placed = (
        P(("dp", "ctx", "tp"), None),
        P(("dp", "ctx", "tp"), None),
        P(("dp", "ctx"), None),
        P(("dp", "ctx"), None),
        P(("dp", "ctx"), None, "tp"),
        P(("dp", "ctx"), None, "tp"),
        P(("dp", "ctx"), "tp", None),
    )
    return jax.shard_map(
        per_device,
        mesh=mesh,
        in_specs=placed,
        out_specs=(
            P(("dp", "ctx", "tp"), None),
            P(("dp", "ctx", "tp"), None),
            P(("dp", "ctx"), None, "tp"),
            P(("dp", "ctx"), None, "tp"),
            P(("dp", "ctx"), "tp", None),
        ),
        check_vma=False,
    )
```
